128 devices in a mesh: row: 8 (over y, x_hi), col: 16 (over z, x_lo, core).
Axes of the slice: x: 4 (x_hi: 2, x_lo: 2; x = x_hi * 2 + x_lo), y: 4, z: 4, core: 2. Of those that a mesh axis runs over, the one named last changes fastest.
Arguments:
- queries: bfloat16 [16384, 1024], P(('row', 'col')), may hold values from -64 to 64
- key_states: bfloat16 [16384, 128], P(('col', 'row')), may hold values from -6 to 6
- value_states: bfloat16 [16384, 128], P(('col', 'row')), may hold values from -6 to 6
- out_grad: bfloat16 [16384, 1024], P(('row', 'col')), may hold values from -6 to 6
- block_order: int32 [256], replicated, may hold values from 0 to 255, each once
Outputs:
- query_grad: bfloat16 [16384, 1024], P(('row', 'col'))
- key_grad: bfloat16 [16384, 128], P(('col', 'row'))
- value_grad: bfloat16 [16384, 128], P(('col', 'row'))
The draws below stay inside these ranges and needn't reach their ends.
Inputs may be any that keep to these rules, and one draw needn't show every extreme that they name: `block_order`: a permutation of 0 to 255.
All inputs are finite; a program needn't handle non-finite values.
Results may differ from the reference program's by a relative error of at most 0.0055.
Values may be sent and summed in bfloat16 or wider, within the bound.
A program may use at most 192 MiB of HBM per device.

```python
import math
import jax
import jax.numpy as jnp
from jax import lax

H = 8
HD = 128
TOKENS = 16384
BLK = 64
NBLK = 256


def pair_draw(key):
    query_key = jax.random.fold_in(key, 11)
    state_key = jax.random.fold_in(key, 12)
    states = jnp.clip(jax.random.normal(state_key, (TOKENS, HD), jnp.float32), -6.0, 6.0)
    vectors = jnp.clip(jax.random.normal(query_key, (TOKENS, H, HD), jnp.float32), -6.0, 6.0)
    return (vectors.reshape(TOKENS, H * HD), states)


def draw_queries(key, part):
    return pair_draw(key)[0].astype(jnp.bfloat16)


def draw_key_states(key, part):
    return pair_draw(key)[1].astype(jnp.bfloat16)


def steps_of(rng, extent, shards, smallest, largest):
    factor_of, own = 1.0, jax.random.fold_in(rng, 6)
    for axis_at, parts in shards:
        heights = jnp.exp(jax.random.uniform(jax.random.fold_in(own, axis_at), (parts,), jnp.float32, smallest / len(shards), largest / len(shards)))
        factor_of = factor_of * jnp.repeat(heights, extent[axis_at] // parts).reshape([-1 if axis == axis_at else 1 for axis in range(len(extent))])
    return factor_of


def noise(own_key, dims, scale, limit, cuts=(), held_as=jnp.bfloat16):
    result = scale * jax.random.normal(own_key, dims, jnp.float32)
    if cuts:
        result = result * steps_of(own_key, dims, cuts, -0.22, 0.18)
    return jnp.clip(result, -limit, limit).astype(held_as)


def setup_inputs(seed: int = 0) -> dict:
    streams_of = jax.random.split(jax.random.key(seed), 6)
    queries = draw_queries(jax.random.fold_in(streams_of[5], 71), 0)
    key_states = draw_key_states(jax.random.fold_in(streams_of[5], 71), 0)
    value_states = noise(streams_of[2], (TOKENS, HD), 1.0, 6.0, ((0, 128),))
    out_grad = noise(streams_of[3], (TOKENS, H * HD), 1.0, 6.0, ((0, 128),))
    block_order = jax.random.permutation(streams_of[4], NBLK).astype(jnp.int32)
    return {"queries": queries, "key_states": key_states, "value_states": value_states, "out_grad": out_grad, "block_order": block_order}


def positions(token_index, block_order):
    block_index = token_index // BLK
    offset = token_index % BLK
    block_ids = jnp.arange(block_order.shape[0], dtype=jnp.int32)
    matches = block_index[:, None] == block_ids[None, :]
    start = lax.optimization_barrier(jnp.sum(jnp.where(matches, block_order[None, :], 0), axis=1)).astype(jnp.int32)
    return start * BLK + offset

def reference(queries, key_states, value_states, out_grad, block_order):
    key_total = queries.shape[0]
    scaling = 1.0 / math.sqrt(HD)
    token_pos = positions(jnp.arange(key_total, dtype=jnp.int32), block_order)
    keys_wide = key_states.astype(jnp.float32)
    values_wide = value_states.astype(jnp.float32)
    block_rows = 256
    blocks = key_total // block_rows
    query_blocks = queries.reshape(blocks, block_rows, H, HD)
    grad_blocks = out_grad.reshape(blocks, block_rows, H, HD)
    pos_blocks = token_pos.reshape(blocks, block_rows)

    def advance(running, pieces):
        key_acc, value_acc = running
        query_blk, grad_blk, pos_blk = pieces
        query_wide = query_blk.astype(jnp.float32)
        grad_wide = grad_blk.astype(jnp.float32)
        scores = jnp.einsum('ihd,jd->hij', query_wide, keys_wide) * scaling
        visible = (token_pos[None, :] <= pos_blk[:, None])[None]
        scores = jnp.where(visible, scores, -1e+30)
        maxima = lax.optimization_barrier(jnp.max(scores, axis=2, keepdims=True))
        summed = lax.optimization_barrier(jnp.sum(jnp.where(visible, jnp.exp(scores - maxima), 0.0), axis=2, keepdims=True))
        logsum = maxima + jnp.log(summed)
        attn_weights = jnp.where(visible, jnp.exp(scores - logsum), 0.0)
        weight_grad = jnp.einsum('ihd,jd->hij', grad_wide, values_wide)
        delta_row = lax.optimization_barrier(jnp.sum(attn_weights * weight_grad, axis=2, keepdims=True))
        dscore = (attn_weights * (weight_grad - delta_row)).astype(jnp.bfloat16)
        dscore = lax.optimization_barrier(dscore).astype(jnp.float32)
        attn_low = attn_weights.astype(jnp.bfloat16)
        attn_low = lax.optimization_barrier(attn_low).astype(jnp.float32)
        query_part = (jnp.einsum('hij,jd->ihd', dscore, keys_wide) * scaling).astype(jnp.bfloat16)
        key_acc = key_acc + jnp.einsum('hij,ihd->jd', dscore, query_wide)
        value_acc = value_acc + jnp.einsum('hij,ihd->jd', attn_low, grad_wide)
        return ((key_acc, value_acc), query_part)
    empty_acc = jnp.zeros((key_total, HD), jnp.float32)
    (key_acc, value_acc), query_parts = lax.scan(advance, (empty_acc, empty_acc), (query_blocks, grad_blocks, pos_blocks))
    query_grad = query_parts.reshape(key_total, H * HD)
    key_grad = (key_acc * scaling).astype(jnp.bfloat16)
    value_grad = value_acc.astype(jnp.bfloat16)
    return (query_grad, key_grad, value_grad)
```

```python
import math

import jax
import jax.numpy as jnp
from jax import lax
from jax.sharding import PartitionSpec as P

H = 8
HD = 128
BLK = 64


def positions(token_index, block_order):
    return block_order[token_index // BLK] * BLK + token_index % BLK


def partial_stats(scores, visible, weight_grad):
    maxima = jnp.max(scores, axis=1)
    expo = jnp.where(visible, jnp.exp(scores - maxima[:, None]), 0.0)
    summed = jnp.sum(expo, axis=1)
    weighted = jnp.sum(expo * weight_grad, axis=1)
    return (maxima, summed, weighted)


def join_stats(former, latter):
    maxima = jnp.maximum(former[0], latter[0])
    first = jnp.exp(former[0] - maxima)
    second = jnp.exp(latter[0] - maxima)
    summed = former[1] * first + latter[1] * second
    weighted = former[2] * first + latter[2] * second
    return (maxima, summed, weighted)


def tile_grid(queries, key_states, value_states, out_grad, block_order, scaling):
    row_amount = lax.axis_size("row")
    col_amount = lax.axis_size("col")
    r = lax.axis_index("row")
    c = lax.axis_index("col")
    local_rows = queries.shape[0]
    query_all = lax.all_gather(queries, "row", axis=0, tiled=True)
    grad_all = lax.all_gather(out_grad, "row", axis=0, tiled=True)
    key_all = lax.all_gather(key_states, "col", axis=0, tiled=True)
    value_all = lax.all_gather(value_states, "col", axis=0, tiled=True)
    q_total = query_all.shape[0]
    k_total = key_all.shape[0]

    qi = jnp.arange(q_total, dtype=jnp.int32)
    q_anchor = ((qi // local_rows) * col_amount + c) * local_rows + qi % local_rows
    query_pos = positions(q_anchor, block_order)
    ki = jnp.arange(k_total, dtype=jnp.int32)
    k_anchor = ((ki // local_rows) * row_amount + r) * local_rows + ki % local_rows
    key_pos = positions(k_anchor, block_order)

    qf = query_all.reshape(q_total * H, HD)
    gf = grad_all.reshape(q_total * H, HD)
    rpos = jnp.repeat(query_pos, H)

    blocks = 2
    block_rows = k_total // blocks
    key_blocks = key_all.reshape(blocks, block_rows, HD)
    value_blocks = value_all.reshape(blocks, block_rows, HD)
    kpos_blocks = key_pos.reshape(blocks, block_rows)

    def scores_of(key_blk, pos_blk):
        s = jnp.dot(qf, key_blk.T, preferred_element_type=jnp.float32) * scaling
        visible = pos_blk[None, :] <= rpos[:, None]
        return jnp.where(visible, s, -1e30), visible

    def stats_pass(running, pieces):
        key_blk, value_blk, pos_blk = pieces
        s, visible = scores_of(key_blk, pos_blk)
        dp = jnp.dot(gf, value_blk.T, preferred_element_type=jnp.float32)
        return (join_stats(running, partial_stats(s, visible, dp)), None)

    rows = q_total * H
    empty = jnp.zeros((rows,), jnp.float32)
    start = (jnp.full((rows,), -1e30, jnp.float32), empty, empty)
    (maxima, summed, weighted), _ = lax.scan(
        stats_pass, start, (key_blocks, value_blocks, kpos_blocks)
    )
    top = lax.pmax(maxima, "row")
    factor = jnp.exp(maxima - top)
    summed, weighted = lax.psum((summed * factor, weighted * factor), "row")
    logsum = top + jnp.log(summed)
    deltas = weighted / summed

    def grad_pass(running, pieces):
        key_blk, value_blk, pos_blk = pieces
        s, visible = scores_of(key_blk, pos_blk)
        attn = jnp.where(visible, jnp.exp(s - logsum[:, None]), 0.0)
        dp = jnp.dot(gf, value_blk.T, preferred_element_type=jnp.float32)
        dscore = (attn * (dp - deltas[:, None])).astype(jnp.bfloat16)
        attn_low = attn.astype(jnp.bfloat16)
        running = running + jnp.dot(dscore, key_blk, preferred_element_type=jnp.float32)
        key_part = jnp.dot(dscore.T, qf, preferred_element_type=jnp.float32)
        value_part = jnp.dot(attn_low.T, gf, preferred_element_type=jnp.float32)
        return (running, (key_part, value_part))

    query_acc, (key_parts, value_parts) = lax.scan(
        grad_pass,
        jnp.zeros((rows, HD), jnp.float32),
        (key_blocks, value_blocks, kpos_blocks),
    )
    key_parts = key_parts.reshape(k_total, HD)
    value_parts = value_parts.reshape(k_total, HD)
    key_grad = lax.psum_scatter(key_parts, "col", scatter_dimension=0, tiled=True)
    value_grad = lax.psum_scatter(value_parts, "col", scatter_dimension=0, tiled=True)
    query_acc = query_acc.reshape(q_total, H * HD)
    query_grad = lax.psum_scatter(query_acc, "row", scatter_dimension=0, tiled=True)
    return (
        (query_grad * scaling).astype(jnp.bfloat16),
        (key_grad * scaling).astype(jnp.bfloat16),
        value_grad.astype(jnp.bfloat16),
    )


def local(queries, key_states, value_states, out_grad, block_order):
    scaling = 1.0 / math.sqrt(key_states.shape[1])
    return tile_grid(queries, key_states, value_states, out_grad, block_order, scaling)


def solution(mesh):
    placed = (
        P(("row", "col"), None),
        P(("col", "row"), None),
        P(("col", "row"), None),
        P(("row", "col"), None),
        P(),
    )
    return jax.shard_map(
        local,
        mesh=mesh,
        in_specs=placed,
        out_specs=(P(("row", "col"), None), P(("col", "row"), None), P(("col", "row"), None)),
        check_vma=False,
    )
```

```python
import math

import jax
import jax.numpy as jnp
from jax import lax
from jax.sharding import PartitionSpec as P

H = 8
HD = 128
BLK = 64


def positions(token_index, block_order):
    block_index = token_index // BLK
    block_ids = jnp.arange(block_order.shape[0], dtype=jnp.int32)
    matches = block_index[:, None] == block_ids[None, :]
    start = jnp.sum(jnp.where(matches, block_order[None, :], 0), axis=1)
    return start * BLK + token_index % BLK


def partial_stats(scores, visible, weight_grad):
    maxima = jnp.max(scores, axis=1)
    expo = jnp.where(visible, jnp.exp(scores - maxima[:, None]), 0.0)
    summed = jnp.sum(expo, axis=1)
    weighted = jnp.sum(expo * weight_grad, axis=1)
    return (maxima, summed, weighted)


def join_stats(former, latter):
    maxima = jnp.maximum(former[0], latter[0])
    first = jnp.exp(former[0] - maxima)
    second = jnp.exp(latter[0] - maxima)
    summed = former[1] * first + latter[1] * second
    weighted = former[2] * first + latter[2] * second
    return (maxima, summed, weighted)


def tile_grid(queries, key_states, value_states, out_grad, block_order, scaling):
    row_amount = lax.axis_size("row")
    col_amount = lax.axis_size("col")
    r = lax.axis_index("row")
    c = lax.axis_index("col")
    local_rows = queries.shape[0]
    width = queries.shape[1]
    pair_all = lax.all_gather(
        jnp.concatenate([queries, out_grad], axis=1), "row", axis=0, tiled=True
    )
    query_all, grad_all = pair_all[:, :width], pair_all[:, width:]
    kv_all = lax.all_gather(
        jnp.concatenate([key_states, value_states], axis=1), "col", axis=0, tiled=True
    )
    key_all, value_all = kv_all[:, :HD], kv_all[:, HD:]
    q_total = query_all.shape[0]
    k_total = key_all.shape[0]

    qi = jnp.arange(q_total, dtype=jnp.int32)
    q_anchor = ((qi // local_rows) * col_amount + c) * local_rows + qi % local_rows
    query_pos = positions(q_anchor, block_order)
    ki = jnp.arange(k_total, dtype=jnp.int32)
    k_anchor = ((ki // local_rows) * row_amount + r) * local_rows + ki % local_rows
    key_pos = positions(k_anchor, block_order)

    qf = query_all.reshape(q_total * H, HD)
    gf = grad_all.reshape(q_total * H, HD)
    rpos = jnp.repeat(query_pos, H)

    blocks = 2
    block_rows = k_total // blocks
    key_blocks = key_all.reshape(blocks, block_rows, HD)
    value_blocks = value_all.reshape(blocks, block_rows, HD)
    kpos_blocks = key_pos.reshape(blocks, block_rows)

    def scores_of(key_blk, pos_blk):
        s = jnp.dot(qf, key_blk.T, preferred_element_type=jnp.float32) * scaling
        visible = pos_blk[None, :] <= rpos[:, None]
        return jnp.where(visible, s, -1e30), visible

    def stats_pass(running, pieces):
        key_blk, value_blk, pos_blk = pieces
        s, visible = scores_of(key_blk, pos_blk)
        dp = jnp.dot(gf, value_blk.T, preferred_element_type=jnp.float32)
        return (join_stats(running, partial_stats(s, visible, dp)), None)

    rows = q_total * H
    empty = jnp.zeros((rows,), jnp.float32)
    start = (jnp.full((rows,), -1e30, jnp.float32), empty, empty)
    (maxima, summed, weighted), _ = lax.scan(
        stats_pass, start, (key_blocks, value_blocks, kpos_blocks)
    )
    gathered = lax.all_gather(jnp.stack([maxima, summed, weighted]), "row", axis=0)
    top = jnp.max(gathered[:, 0], axis=0)
    factor = jnp.exp(gathered[:, 0] - top[None])
    summed = jnp.sum(gathered[:, 1] * factor, axis=0)
    weighted = jnp.sum(gathered[:, 2] * factor, axis=0)
    logsum = top + jnp.log(summed)
    deltas = weighted / summed

    def grad_pass(running, pieces):
        key_blk, value_blk, pos_blk = pieces
        s, visible = scores_of(key_blk, pos_blk)
        attn = jnp.where(visible, jnp.exp(s - logsum[:, None]), 0.0)
        dp = jnp.dot(gf, value_blk.T, preferred_element_type=jnp.float32)
        dscore = (attn * (dp - deltas[:, None])).astype(jnp.bfloat16)
        attn_low = attn.astype(jnp.bfloat16)
        running = running + jnp.dot(dscore, key_blk, preferred_element_type=jnp.float32)
        key_part = jnp.dot(dscore.T, qf, preferred_element_type=jnp.float32)
        value_part = jnp.dot(attn_low.T, gf, preferred_element_type=jnp.float32)
        return (running, (key_part, value_part))

    query_acc, (key_parts, value_parts) = lax.scan(
        grad_pass,
        jnp.zeros((rows, HD), jnp.float32),
        (key_blocks, value_blocks, kpos_blocks),
    )
    kv_parts = jnp.concatenate(
        [key_parts.reshape(k_total, HD), value_parts.reshape(k_total, HD)], axis=1
    )
    kv_grad = lax.psum_scatter(kv_parts, "col", scatter_dimension=0, tiled=True)
    key_grad, value_grad = kv_grad[:, :HD], kv_grad[:, HD:]
    query_acc = query_acc.reshape(q_total, H * HD)
    query_grad = lax.psum_scatter(query_acc, "row", scatter_dimension=0, tiled=True)
    return (
        (query_grad * scaling).astype(jnp.bfloat16),
        (key_grad * scaling).astype(jnp.bfloat16),
        value_grad.astype(jnp.bfloat16),
    )


def local(queries, key_states, value_states, out_grad, block_order):
    scaling = 1.0 / math.sqrt(key_states.shape[1])
    return tile_grid(queries, key_states, value_states, out_grad, block_order, scaling)


def solution(mesh):
    placed = (
        P(("row", "col"), None),
        P(("col", "row"), None),
        P(("col", "row"), None),
        P(("row", "col"), None),
        P(),
    )
    return jax.shard_map(
        local,
        mesh=mesh,
        in_specs=placed,
        out_specs=(P(("row", "col"), None), P(("col", "row"), None), P(("col", "row"), None)),
        check_vma=False,
    )
```

```python
import math
import os

import jax
import jax.numpy as jnp
from jax import lax
from jax.experimental import pallas as pl
from jax.experimental.pallas import tpu as pltpu
from jax.sharding import PartitionSpec as P

H = 8
HD = 128
BLK = 64
TQ = 256
INTERPRET = bool(os.environ.get("SOL_INTERPRET"))


def positions(token_index, block_order):
    block_index = token_index // BLK
    block_ids = jnp.arange(block_order.shape[0], dtype=jnp.int32)
    matches = block_index[:, None] == block_ids[None, :]
    start = jnp.sum(jnp.where(matches, block_order[None, :], 0), axis=1)
    return start * BLK + token_index % BLK


def _nt(a, b):
    return lax.dot_general(a, b, (((1,), (1,)), ((), ())), preferred_element_type=jnp.float32)


def _tn(a, b):
    return lax.dot_general(a, b, (((0,), (0,)), ((), ())), preferred_element_type=jnp.float32)


def stats_call(qf, gf, keys, values, rpos, kpos, scaling):
    rows = qf.shape[0]
    n = keys.shape[0]

    def kernel(q_ref, g_ref, k_ref, v_ref, rp_ref, kp_ref, m_ref, l_ref, w_ref):
        s = _nt(q_ref[...], k_ref[...]) * scaling
        vis = kp_ref[...] <= rp_ref[...]
        s = jnp.where(vis, s, -1e30)
        m = jnp.max(s, axis=1, keepdims=True)
        e = jnp.where(vis, jnp.exp(s - m), 0.0)
        dp = _nt(g_ref[...], v_ref[...])
        m_ref[...] = m
        l_ref[...] = jnp.sum(e, axis=1, keepdims=True)
        w_ref[...] = jnp.sum(e * dp, axis=1, keepdims=True)

    row_blk = pl.BlockSpec((TQ, HD), lambda i: (i, 0))
    full = pl.BlockSpec((n, HD), lambda i: (0, 0))
    col_blk = pl.BlockSpec((TQ, 1), lambda i: (i, 0))
    out = jax.ShapeDtypeStruct((rows, 1), jnp.float32)
    return pl.pallas_call(
        kernel,
        grid=(rows // TQ,),
        in_specs=[row_blk, row_blk, full, full, col_blk, pl.BlockSpec((1, n), lambda i: (0, 0))],
        out_specs=[col_blk, col_blk, col_blk],
        out_shape=[out, out, out],
        compiler_params=pltpu.CompilerParams(dimension_semantics=("arbitrary",)),
        interpret=INTERPRET,
    )(qf, gf, keys, values, rpos, kpos)


def grad_call(qf, gf, keys, values, rpos, kpos, logsum, deltas, scaling):
    rows = qf.shape[0]
    n = keys.shape[0]

    def kernel(q_ref, g_ref, k_ref, v_ref, rp_ref, kp_ref, ls_ref, dl_ref, dq_ref, dk_ref, dv_ref):
        i = pl.program_id(0)
        q = q_ref[...]
        g = g_ref[...]
        k = k_ref[...]
        s = _nt(q, k) * scaling
        vis = kp_ref[...] <= rp_ref[...]
        s = jnp.where(vis, s, -1e30)
        p = jnp.where(vis, jnp.exp(s - ls_ref[...]), 0.0)
        dp = _nt(g, v_ref[...])
        ds = (p * (dp - dl_ref[...])).astype(jnp.bfloat16)
        pb = p.astype(jnp.bfloat16)
        dq_ref[...] = jnp.dot(ds, k, preferred_element_type=jnp.float32)

        @pl.when(i == 0)
        def _():
            dk_ref[...] = jnp.zeros_like(dk_ref)
            dv_ref[...] = jnp.zeros_like(dv_ref)

        dk_ref[...] += _tn(ds, q)
        dv_ref[...] += _tn(pb, g)

    row_blk = pl.BlockSpec((TQ, HD), lambda i: (i, 0))
    full = pl.BlockSpec((n, HD), lambda i: (0, 0))
    col_blk = pl.BlockSpec((TQ, 1), lambda i: (i, 0))
    return pl.pallas_call(
        kernel,
        grid=(rows // TQ,),
        in_specs=[
            row_blk, row_blk, full, full, col_blk,
            pl.BlockSpec((1, n), lambda i: (0, 0)), col_blk, col_blk,
        ],
        out_specs=[row_blk, full, full],
        out_shape=[
            jax.ShapeDtypeStruct((rows, HD), jnp.float32),
            jax.ShapeDtypeStruct((n, HD), jnp.float32),
            jax.ShapeDtypeStruct((n, HD), jnp.float32),
        ],
        compiler_params=pltpu.CompilerParams(dimension_semantics=("arbitrary",)),
        interpret=INTERPRET,
    )(qf, gf, keys, values, rpos, kpos, logsum, deltas)


def tile_grid(queries, key_states, value_states, out_grad, block_order, scaling):
    row_amount = lax.axis_size("row")
    col_amount = lax.axis_size("col")
    r = lax.axis_index("row")
    c = lax.axis_index("col")
    local_rows = queries.shape[0]
    width = queries.shape[1]
    pair_all = lax.all_gather(
        jnp.concatenate([queries, out_grad], axis=1), "row", axis=0, tiled=True
    )
    query_all, grad_all = pair_all[:, :width], pair_all[:, width:]
    kv_all = lax.all_gather(
        jnp.concatenate([key_states, value_states], axis=1), "col", axis=0, tiled=True
    )
    key_all, value_all = kv_all[:, :HD], kv_all[:, HD:]
    q_total = query_all.shape[0]
    k_total = key_all.shape[0]

    qi = jnp.arange(q_total, dtype=jnp.int32)
    q_anchor = ((qi // local_rows) * col_amount + c) * local_rows + qi % local_rows
    query_pos = positions(q_anchor, block_order)
    ki = jnp.arange(k_total, dtype=jnp.int32)
    k_anchor = ((ki // local_rows) * row_amount + r) * local_rows + ki % local_rows
    key_pos = positions(k_anchor, block_order)

    rows = q_total * H
    qf = query_all.reshape(rows, HD)
    gf = grad_all.reshape(rows, HD)
    rpos = jnp.repeat(query_pos, H).reshape(rows, 1)
    kpos = key_pos.reshape(1, k_total)

    maxima, summed, weighted = stats_call(qf, gf, key_all, value_all, rpos, kpos, scaling)
    gathered = lax.all_gather(
        jnp.stack([maxima[:, 0], summed[:, 0], weighted[:, 0]]), "row", axis=0
    )
    top = jnp.max(gathered[:, 0], axis=0)
    factor = jnp.exp(gathered[:, 0] - top[None])
    summed = jnp.sum(gathered[:, 1] * factor, axis=0)
    weighted = jnp.sum(gathered[:, 2] * factor, axis=0)
    logsum = (top + jnp.log(summed)).reshape(rows, 1)
    deltas = (weighted / summed).reshape(rows, 1)

    query_acc, key_parts, value_parts = grad_call(
        qf, gf, key_all, value_all, rpos, kpos, logsum, deltas, scaling
    )
    kv_parts = jnp.concatenate(
        [key_parts.reshape(k_total, HD), value_parts.reshape(k_total, HD)], axis=1
    )
    kv_grad = lax.psum_scatter(kv_parts, "col", scatter_dimension=0, tiled=True)
    key_grad, value_grad = kv_grad[:, :HD], kv_grad[:, HD:]
    query_acc = query_acc.reshape(q_total, H * HD)
    query_grad = lax.psum_scatter(query_acc, "row", scatter_dimension=0, tiled=True)
    return (
        (query_grad * scaling).astype(jnp.bfloat16),
        (key_grad * scaling).astype(jnp.bfloat16),
        value_grad.astype(jnp.bfloat16),
    )


def local(queries, key_states, value_states, out_grad, block_order):
    scaling = 1.0 / math.sqrt(key_states.shape[1])
    return tile_grid(queries, key_states, value_states, out_grad, block_order, scaling)


def solution(mesh):
    placed = (
        P(("row", "col"), None),
        P(("col", "row"), None),
        P(("col", "row"), None),
        P(("row", "col"), None),
        P(),
    )
    return jax.shard_map(
        local,
        mesh=mesh,
        in_specs=placed,
        out_specs=(P(("row", "col"), None), P(("col", "row"), None), P(("col", "row"), None)),
        check_vma=False,
    )
```

```python
import math
import os

import jax
import jax.numpy as jnp
from jax import lax
from jax.experimental import pallas as pl
from jax.experimental.pallas import tpu as pltpu
from jax.sharding import PartitionSpec as P

H = 8
HD = 128
BLK = 64
TQ = 256
INTERPRET = bool(os.environ.get("SOL_INTERPRET"))


def positions(token_index, block_order):
    block_index = token_index // BLK
    block_ids = jnp.arange(block_order.shape[0], dtype=jnp.int32)
    matches = block_index[:, None] == block_ids[None, :]
    start = jnp.sum(jnp.where(matches, block_order[None, :], 0), axis=1)
    return start * BLK + token_index % BLK


def _nt(a, b):
    return lax.dot_general(a, b, (((1,), (1,)), ((), ())), preferred_element_type=jnp.float32)


def _tn(a, b):
    return lax.dot_general(a, b, (((0,), (0,)), ((), ())), preferred_element_type=jnp.float32)


def stats_call(pair_all, kv_all, qpos, kpos, scaling):
    q_total = pair_all.shape[0]
    n = kv_all.shape[0]

    def kernel(q_ref, g_ref, k_ref, v_ref, qp_ref, kp_ref, m_ref, l_ref, w_ref):
        s = _nt(k_ref[...], q_ref[...]) * scaling
        vis = kp_ref[...] <= qp_ref[...]
        s = jnp.where(vis, s, -1e30)
        m = jnp.max(s, axis=0, keepdims=True)
        e = jnp.where(vis, jnp.exp(s - m), 0.0)
        dp = _nt(v_ref[...], g_ref[...])
        m_ref[...] = m
        l_ref[...] = jnp.sum(e, axis=0, keepdims=True)
        w_ref[...] = jnp.sum(e * dp, axis=0, keepdims=True)

    stat_blk = pl.BlockSpec((None, 1, TQ), lambda b, h: (h, 0, b))
    out = jax.ShapeDtypeStruct((H, 1, q_total), jnp.float32)
    return pl.pallas_call(
        kernel,
        grid=(q_total // TQ, H),
        in_specs=[
            pl.BlockSpec((TQ, HD), lambda b, h: (b, h)),
            pl.BlockSpec((TQ, HD), lambda b, h: (b, H + h)),
            pl.BlockSpec((n, HD), lambda b, h: (0, 0)),
            pl.BlockSpec((n, HD), lambda b, h: (0, 1)),
            pl.BlockSpec((1, TQ), lambda b, h: (0, b)),
            pl.BlockSpec((n, 1), lambda b, h: (0, 0)),
        ],
        out_specs=[stat_blk, stat_blk, stat_blk],
        out_shape=[out, out, out],
        compiler_params=pltpu.CompilerParams(dimension_semantics=("arbitrary", "arbitrary")),
        interpret=INTERPRET,
    )(pair_all, pair_all, kv_all, kv_all, qpos, kpos)


def grad_call(pair_all, kv_all, qpos, kpos, logsum, deltas, scaling):
    q_total = pair_all.shape[0]
    n = kv_all.shape[0]

    def kernel(q_ref, g_ref, k_ref, v_ref, qp_ref, kp_ref, ls_ref, dl_ref, dq_ref, kv_ref):
        first = (pl.program_id(0) == 0) & (pl.program_id(1) == 0)
        q = q_ref[...]
        g = g_ref[...]
        k = k_ref[...]
        s = _nt(k, q) * scaling
        vis = kp_ref[...] <= qp_ref[...]
        s = jnp.where(vis, s, -1e30)
        p = jnp.where(vis, jnp.exp(s - ls_ref[...]), 0.0)
        dp = _nt(v_ref[...], g)
        ds = (p * (dp - dl_ref[...])).astype(jnp.bfloat16)
        pb = p.astype(jnp.bfloat16)
        dq_ref[...] = _tn(ds, k)

        @pl.when(first)
        def _():
            kv_ref[...] = jnp.zeros_like(kv_ref)

        kv_ref[:, :HD] += jnp.dot(ds, q, preferred_element_type=jnp.float32)
        kv_ref[:, HD:] += jnp.dot(pb, g, preferred_element_type=jnp.float32)

    stat_blk = pl.BlockSpec((None, 1, TQ), lambda b, h: (h, 0, b))
    return pl.pallas_call(
        kernel,
        grid=(q_total // TQ, H),
        in_specs=[
            pl.BlockSpec((TQ, HD), lambda b, h: (b, h)),
            pl.BlockSpec((TQ, HD), lambda b, h: (b, H + h)),
            pl.BlockSpec((n, HD), lambda b, h: (0, 0)),
            pl.BlockSpec((n, HD), lambda b, h: (0, 1)),
            pl.BlockSpec((1, TQ), lambda b, h: (0, b)),
            pl.BlockSpec((n, 1), lambda b, h: (0, 0)),
            stat_blk,
            stat_blk,
        ],
        out_specs=[
            pl.BlockSpec((TQ, HD), lambda b, h: (b, h)),
            pl.BlockSpec((n, 2 * HD), lambda b, h: (0, 0)),
        ],
        out_shape=[
            jax.ShapeDtypeStruct((q_total, H * HD), jnp.float32),
            jax.ShapeDtypeStruct((n, 2 * HD), jnp.float32),
        ],
        compiler_params=pltpu.CompilerParams(dimension_semantics=("arbitrary", "arbitrary")),
        interpret=INTERPRET,
    )(pair_all, pair_all, kv_all, kv_all, qpos, kpos, logsum, deltas)


def tile_grid(queries, key_states, value_states, out_grad, block_order, scaling):
    row_amount = lax.axis_size("row")
    col_amount = lax.axis_size("col")
    r = lax.axis_index("row")
    c = lax.axis_index("col")
    local_rows = queries.shape[0]
    pair_all = lax.all_gather(
        jnp.concatenate([queries, out_grad], axis=1), "row", axis=0, tiled=True
    )
    kv_all = lax.all_gather(
        jnp.concatenate([key_states, value_states], axis=1), "col", axis=0, tiled=True
    )
    q_total = pair_all.shape[0]
    k_total = kv_all.shape[0]

    qi = jnp.arange(q_total, dtype=jnp.int32)
    q_anchor = ((qi // local_rows) * col_amount + c) * local_rows + qi % local_rows
    qpos = positions(q_anchor, block_order).reshape(1, q_total)
    ki = jnp.arange(k_total, dtype=jnp.int32)
    k_anchor = ((ki // local_rows) * row_amount + r) * local_rows + ki % local_rows
    kpos = positions(k_anchor, block_order).reshape(k_total, 1)

    maxima, summed, weighted = stats_call(pair_all, kv_all, qpos, kpos, scaling)
    stacked = jnp.stack([maxima[:, 0], summed[:, 0], weighted[:, 0]])
    gathered = lax.all_gather(stacked, "row", axis=0, tiled=True)
    gathered = gathered.reshape(row_amount, 3, H, q_total)
    top = jnp.max(gathered[:, 0], axis=0)
    factor = jnp.exp(gathered[:, 0] - top[None])
    summed = jnp.sum(gathered[:, 1] * factor, axis=0)
    weighted = jnp.sum(gathered[:, 2] * factor, axis=0)
    logsum = (top + jnp.log(summed)).reshape(H, 1, q_total)
    deltas = (weighted / summed).reshape(H, 1, q_total)

    query_acc, kv_parts = grad_call(pair_all, kv_all, qpos, kpos, logsum, deltas, scaling)
    kv_grad = lax.psum_scatter(kv_parts, "col", scatter_dimension=0, tiled=True)
    key_grad, value_grad = kv_grad[:, :HD], kv_grad[:, HD:]
    query_grad = lax.psum_scatter(query_acc, "row", scatter_dimension=0, tiled=True)
    return (
        (query_grad * scaling).astype(jnp.bfloat16),
        (key_grad * scaling).astype(jnp.bfloat16),
        value_grad.astype(jnp.bfloat16),
    )


def local(queries, key_states, value_states, out_grad, block_order):
    scaling = 1.0 / math.sqrt(key_states.shape[1])
    return tile_grid(queries, key_states, value_states, out_grad, block_order, scaling)


def solution(mesh):
    placed = (
        P(("row", "col"), None),
        P(("col", "row"), None),
        P(("col", "row"), None),
        P(("row", "col"), None),
        P(),
    )
    return jax.shard_map(
        local,
        mesh=mesh,
        in_specs=placed,
        out_specs=(P(("row", "col"), None), P(("col", "row"), None), P(("col", "row"), None)),
        check_vma=False,
    )
```

```python
import math
import os

import jax
import jax.numpy as jnp
from jax import lax
from jax.experimental import pallas as pl
from jax.experimental.pallas import tpu as pltpu
from jax.sharding import PartitionSpec as P

H = 8
HD = 128
BLK = 64
TQ = 256
INTERPRET = bool(os.environ.get("SOL_INTERPRET"))


def positions(token_index, block_order):
    block_index = token_index // BLK
    block_ids = jnp.arange(block_order.shape[0], dtype=jnp.int32)
    matches = block_index[:, None] == block_ids[None, :]
    start = jnp.sum(jnp.where(matches, block_order[None, :], 0), axis=1)
    return start * BLK + token_index % BLK


def _nt(a, b):
    return lax.dot_general(a, b, (((1,), (1,)), ((), ())), preferred_element_type=jnp.float32)


def _tn(a, b):
    return lax.dot_general(a, b, (((0,), (0,)), ((), ())), preferred_element_type=jnp.float32)


def stats_call(pair_all, kv_all, qpos, kpos, scaling):
    q_total = pair_all.shape[0]
    n = kv_all.shape[0]

    def kernel(q_ref, g_ref, k_ref, v_ref, qp_ref, kp_ref, m_ref, l_ref, w_ref):
        s = _nt(k_ref[...], q_ref[...]) * scaling
        vis = kp_ref[...] <= qp_ref[...]
        s = jnp.where(vis, s, -1e30)
        m = jnp.max(s, axis=0, keepdims=True)
        e = jnp.where(vis, jnp.exp(s - m), 0.0)
        dp = _nt(v_ref[...], g_ref[...])
        m_ref[...] = m
        l_ref[...] = jnp.sum(e, axis=0, keepdims=True)
        w_ref[...] = jnp.sum(e * dp, axis=0, keepdims=True)

    stat_blk = pl.BlockSpec((None, 1, TQ), lambda b, h: (h, 0, b))
    out = jax.ShapeDtypeStruct((H, 1, q_total), jnp.float32)
    return pl.pallas_call(
        kernel,
        grid=(q_total // TQ, H),
        in_specs=[
            pl.BlockSpec((TQ, HD), lambda b, h: (b, h)),
            pl.BlockSpec((TQ, HD), lambda b, h: (b, H + h)),
            pl.BlockSpec((n, HD), lambda b, h: (0, 0)),
            pl.BlockSpec((n, HD), lambda b, h: (0, 1)),
            pl.BlockSpec((1, TQ), lambda b, h: (0, b)),
            pl.BlockSpec((n, 1), lambda b, h: (0, 0)),
        ],
        out_specs=[stat_blk, stat_blk, stat_blk],
        out_shape=[out, out, out],
        compiler_params=pltpu.CompilerParams(dimension_semantics=("arbitrary", "arbitrary")),
        interpret=INTERPRET,
    )(pair_all, pair_all, kv_all, kv_all, qpos, kpos)


def grad_call(pair_all, kv_all, qpos, kpos, logsum, deltas, scaling):
    q_total = pair_all.shape[0]
    n = kv_all.shape[0]

    def kernel(q_ref, g_ref, k_ref, v_ref, qp_ref, kp_ref, ls_ref, dl_ref, dq_ref, kv_ref):
        first = (pl.program_id(0) == 0) & (pl.program_id(1) == 0)
        q = q_ref[...]
        g = g_ref[...]
        k = k_ref[...]
        s = _nt(k, q) * scaling
        vis = kp_ref[...] <= qp_ref[...]
        s = jnp.where(vis, s, -1e30)
        p = jnp.where(vis, jnp.exp(s - ls_ref[...]), 0.0)
        dp = _nt(v_ref[...], g)
        ds = (p * (dp - dl_ref[...])).astype(jnp.bfloat16)
        pb = p.astype(jnp.bfloat16)
        dq_ref[...] = _tn(ds, k)

        @pl.when(first)
        def _():
            kv_ref[...] = jnp.zeros_like(kv_ref)

        kv_ref[:, :HD] += jnp.dot(ds, q, preferred_element_type=jnp.float32)
        kv_ref[:, HD:] += jnp.dot(pb, g, preferred_element_type=jnp.float32)

    stat_blk = pl.BlockSpec((None, 1, TQ), lambda b, h: (h, 0, b))
    return pl.pallas_call(
        kernel,
        grid=(q_total // TQ, H),
        in_specs=[
            pl.BlockSpec((TQ, HD), lambda b, h: (b, h)),
            pl.BlockSpec((TQ, HD), lambda b, h: (b, H + h)),
            pl.BlockSpec((n, HD), lambda b, h: (0, 0)),
            pl.BlockSpec((n, HD), lambda b, h: (0, 1)),
            pl.BlockSpec((1, TQ), lambda b, h: (0, b)),
            pl.BlockSpec((n, 1), lambda b, h: (0, 0)),
            stat_blk,
            stat_blk,
        ],
        out_specs=[
            pl.BlockSpec((TQ, HD), lambda b, h: (b, h)),
            pl.BlockSpec((n, 2 * HD), lambda b, h: (0, 0)),
        ],
        out_shape=[
            jax.ShapeDtypeStruct((q_total, H * HD), jnp.float32),
            jax.ShapeDtypeStruct((n, 2 * HD), jnp.float32),
        ],
        compiler_params=pltpu.CompilerParams(dimension_semantics=("arbitrary", "arbitrary")),
        interpret=INTERPRET,
    )(pair_all, pair_all, kv_all, kv_all, qpos, kpos, logsum, deltas)


def tile_grid(queries, key_states, value_states, out_grad, block_order, scaling):
    row_amount = lax.axis_size("row")
    col_amount = lax.axis_size("col")
    r = lax.axis_index("row")
    c = lax.axis_index("col")
    local_rows = queries.shape[0]
    pair = jnp.concatenate([queries, out_grad], axis=1)
    kv_all = lax.all_gather(
        jnp.concatenate([key_states, value_states], axis=1), "col", axis=0, tiled=True
    )
    k_total = kv_all.shape[0]
    ki = jnp.arange(k_total, dtype=jnp.int32)
    k_anchor = ((ki // local_rows) * row_amount + r) * local_rows + ki % local_rows
    kpos = positions(k_anchor, block_order).reshape(k_total, 1)

    pieces = 2
    piece = local_rows // pieces
    query_parts = []
    kv_parts = None
    for part in range(pieces):
        pair_all = lax.all_gather(
            pair[part * piece:(part + 1) * piece], "row", axis=0, tiled=True
        )
        q_total = pair_all.shape[0]
        qi = jnp.arange(q_total, dtype=jnp.int32)
        q_anchor = (
            ((qi // piece) * col_amount + c) * local_rows + part * piece + qi % piece
        )
        qpos = positions(q_anchor, block_order).reshape(1, q_total)

        maxima, summed, weighted = stats_call(pair_all, kv_all, qpos, kpos, scaling)
        stacked = jnp.stack([maxima[:, 0], summed[:, 0], weighted[:, 0]])
        gathered = lax.all_gather(stacked, "row", axis=0, tiled=True)
        gathered = gathered.reshape(row_amount, 3, H, q_total)
        top = jnp.max(gathered[:, 0], axis=0)
        factor = jnp.exp(gathered[:, 0] - top[None])
        summed = jnp.sum(gathered[:, 1] * factor, axis=0)
        weighted = jnp.sum(gathered[:, 2] * factor, axis=0)
        logsum = (top + jnp.log(summed)).reshape(H, 1, q_total)
        deltas = (weighted / summed).reshape(H, 1, q_total)

        query_acc, kv_piece = grad_call(
            pair_all, kv_all, qpos, kpos, logsum, deltas, scaling
        )
        query_parts.append(
            lax.psum_scatter(query_acc, "row", scatter_dimension=0, tiled=True)
        )
        kv_parts = kv_piece if kv_parts is None else kv_parts + kv_piece
    kv_grad = lax.psum_scatter(kv_parts, "col", scatter_dimension=0, tiled=True)
    key_grad, value_grad = kv_grad[:, :HD], kv_grad[:, HD:]
    query_grad = jnp.concatenate(query_parts, axis=0)
    return (
        (query_grad * scaling).astype(jnp.bfloat16),
        (key_grad * scaling).astype(jnp.bfloat16),
        value_grad.astype(jnp.bfloat16),
    )


def local(queries, key_states, value_states, out_grad, block_order):
    scaling = 1.0 / math.sqrt(key_states.shape[1])
    return tile_grid(queries, key_states, value_states, out_grad, block_order, scaling)


def solution(mesh):
    placed = (
        P(("row", "col"), None),
        P(("col", "row"), None),
        P(("col", "row"), None),
        P(("row", "col"), None),
        P(),
    )
    return jax.shard_map(
        local,
        mesh=mesh,
        in_specs=placed,
        out_specs=(P(("row", "col"), None), P(("col", "row"), None), P(("col", "row"), None)),
        check_vma=False,
    )
```

```python
import math
import os

import jax
import jax.numpy as jnp
from jax import lax
from jax.experimental import pallas as pl
from jax.experimental.pallas import tpu as pltpu
from jax.sharding import PartitionSpec as P

H = 8
HD = 128
BLK = 64
TQ = 256
INTERPRET = bool(os.environ.get("SOL_INTERPRET"))


def positions(token_index, block_order):
    block_index = token_index // BLK
    block_ids = jnp.arange(block_order.shape[0], dtype=jnp.int32)
    matches = block_index[:, None] == block_ids[None, :]
    start = jnp.sum(jnp.where(matches, block_order[None, :], 0), axis=1)
    return start * BLK + token_index % BLK


def _nt(a, b):
    return lax.dot_general(a, b, (((1,), (1,)), ((), ())), preferred_element_type=jnp.float32)


def _tn(a, b):
    return lax.dot_general(a, b, (((0,), (0,)), ((), ())), preferred_element_type=jnp.float32)


def stats_call(pair_all, kv_all, qpos, kpos, scaling):
    q_total = pair_all.shape[0]
    n = kv_all.shape[0]

    def kernel(q_ref, g_ref, k_ref, v_ref, qp_ref, kp_ref, m_ref, l_ref, w_ref):
        s = _nt(k_ref[...], q_ref[...]) * scaling
        vis = kp_ref[...] <= qp_ref[...]
        s = jnp.where(vis, s, -1e30)
        m = jnp.max(s, axis=0, keepdims=True)
        e = jnp.exp(s - jnp.maximum(m, -1e29))
        dp = _nt(v_ref[...], g_ref[...])
        m_ref[...] = m
        l_ref[...] = jnp.sum(e, axis=0, keepdims=True)
        w_ref[...] = jnp.sum(e * dp, axis=0, keepdims=True)

    stat_blk = pl.BlockSpec((None, 1, TQ), lambda b, h: (h, 0, b))
    out = jax.ShapeDtypeStruct((H, 1, q_total), jnp.float32)
    return pl.pallas_call(
        kernel,
        grid=(q_total // TQ, H),
        in_specs=[
            pl.BlockSpec((TQ, HD), lambda b, h: (b, h)),
            pl.BlockSpec((TQ, HD), lambda b, h: (b, H + h)),
            pl.BlockSpec((n, HD), lambda b, h: (0, 0)),
            pl.BlockSpec((n, HD), lambda b, h: (0, 1)),
            pl.BlockSpec((1, TQ), lambda b, h: (0, b)),
            pl.BlockSpec((n, 1), lambda b, h: (0, 0)),
        ],
        out_specs=[stat_blk, stat_blk, stat_blk],
        out_shape=[out, out, out],
        compiler_params=pltpu.CompilerParams(dimension_semantics=("arbitrary", "arbitrary")),
        interpret=INTERPRET,
    )(pair_all, pair_all, kv_all, kv_all, qpos, kpos)


def grad_call(pair_all, kv_all, qpos, kpos, logsum, deltas, scaling):
    q_total = pair_all.shape[0]
    n = kv_all.shape[0]

    def kernel(q_ref, g_ref, k_ref, v_ref, qp_ref, kp_ref, ls_ref, dl_ref, dq_ref, kv_ref):
        first = (pl.program_id(0) == 0) & (pl.program_id(1) == 0)
        q = q_ref[...]
        g = g_ref[...]
        k = k_ref[...]
        s = _nt(k, q) * scaling
        vis = kp_ref[...] <= qp_ref[...]
        p = jnp.exp(jnp.where(vis, s, -1e30) - ls_ref[...])
        dp = _nt(v_ref[...], g)
        ds = (p * (dp - dl_ref[...])).astype(jnp.bfloat16)
        pb = p.astype(jnp.bfloat16)
        dq_ref[...] = _tn(ds, k)

        @pl.when(first)
        def _():
            kv_ref[...] = jnp.zeros_like(kv_ref)

        kv_ref[:, :HD] += jnp.dot(ds, q, preferred_element_type=jnp.float32)
        kv_ref[:, HD:] += jnp.dot(pb, g, preferred_element_type=jnp.float32)

    stat_blk = pl.BlockSpec((None, 1, TQ), lambda b, h: (h, 0, b))
    return pl.pallas_call(
        kernel,
        grid=(q_total // TQ, H),
        in_specs=[
            pl.BlockSpec((TQ, HD), lambda b, h: (b, h)),
            pl.BlockSpec((TQ, HD), lambda b, h: (b, H + h)),
            pl.BlockSpec((n, HD), lambda b, h: (0, 0)),
            pl.BlockSpec((n, HD), lambda b, h: (0, 1)),
            pl.BlockSpec((1, TQ), lambda b, h: (0, b)),
            pl.BlockSpec((n, 1), lambda b, h: (0, 0)),
            stat_blk,
            stat_blk,
        ],
        out_specs=[
            pl.BlockSpec((TQ, HD), lambda b, h: (b, h)),
            pl.BlockSpec((n, 2 * HD), lambda b, h: (0, 0)),
        ],
        out_shape=[
            jax.ShapeDtypeStruct((q_total, H * HD), jnp.float32),
            jax.ShapeDtypeStruct((n, 2 * HD), jnp.float32),
        ],
        compiler_params=pltpu.CompilerParams(dimension_semantics=("arbitrary", "arbitrary")),
        interpret=INTERPRET,
    )(pair_all, pair_all, kv_all, kv_all, qpos, kpos, logsum, deltas)


def tile_grid(queries, key_states, value_states, out_grad, block_order, scaling):
    row_amount = lax.axis_size("row")
    col_amount = lax.axis_size("col")
    r = lax.axis_index("row")
    c = lax.axis_index("col")
    local_rows = queries.shape[0]
    pair_all = lax.all_gather(
        jnp.concatenate([queries, out_grad], axis=1), "row", axis=0, tiled=True
    )
    kv_all = lax.all_gather(
        jnp.concatenate([key_states, value_states], axis=1), "col", axis=0, tiled=True
    )
    q_total = pair_all.shape[0]
    k_total = kv_all.shape[0]

    qi = jnp.arange(q_total, dtype=jnp.int32)
    q_anchor = ((qi // local_rows) * col_amount + c) * local_rows + qi % local_rows
    qpos = positions(q_anchor, block_order).reshape(1, q_total)
    ki = jnp.arange(k_total, dtype=jnp.int32)
    k_anchor = ((ki // local_rows) * row_amount + r) * local_rows + ki % local_rows
    kpos = positions(k_anchor, block_order).reshape(k_total, 1)

    maxima, summed, weighted = stats_call(pair_all, kv_all, qpos, kpos, scaling)
    stacked = jnp.stack([maxima[:, 0], summed[:, 0], weighted[:, 0]])
    gathered = lax.all_gather(stacked, "row", axis=0, tiled=True)
    gathered = gathered.reshape(row_amount, 3, H, q_total)
    top = jnp.max(gathered[:, 0], axis=0)
    factor = jnp.exp(gathered[:, 0] - top[None])
    summed = jnp.sum(gathered[:, 1] * factor, axis=0)
    weighted = jnp.sum(gathered[:, 2] * factor, axis=0)
    logsum = (top + jnp.log(summed)).reshape(H, 1, q_total)
    deltas = (weighted / summed).reshape(H, 1, q_total)

    query_acc, kv_parts = grad_call(pair_all, kv_all, qpos, kpos, logsum, deltas, scaling)
    kv_grad = lax.psum_scatter(kv_parts, "col", scatter_dimension=0, tiled=True)
    key_grad, value_grad = kv_grad[:, :HD], kv_grad[:, HD:]
    exchanged = lax.all_to_all(query_acc, "row", 0, 0, tiled=True)
    query_grad = jnp.sum(exchanged.reshape(row_amount, local_rows, H * HD), axis=0)
    return (
        (query_grad * scaling).astype(jnp.bfloat16),
        (key_grad * scaling).astype(jnp.bfloat16),
        value_grad.astype(jnp.bfloat16),
    )


def local(queries, key_states, value_states, out_grad, block_order):
    scaling = 1.0 / math.sqrt(key_states.shape[1])
    return tile_grid(queries, key_states, value_states, out_grad, block_order, scaling)


def solution(mesh):
    placed = (
        P(("row", "col"), None),
        P(("col", "row"), None),
        P(("col", "row"), None),
        P(("row", "col"), None),
        P(),
    )
    return jax.shard_map(
        local,
        mesh=mesh,
        in_specs=placed,
        out_specs=(P(("row", "col"), None), P(("col", "row"), None), P(("col", "row"), None)),
        check_vma=False,
    )
```

```python
import math
import os

import jax
import jax.numpy as jnp
from jax import lax
from jax.experimental import pallas as pl
from jax.experimental.pallas import tpu as pltpu
from jax.sharding import PartitionSpec as P

H = 8
HD = 128
BLK = 64
TQ = 256
INTERPRET = bool(os.environ.get("SOL_INTERPRET"))


def positions(token_index, block_order):
    block_index = token_index // BLK
    block_ids = jnp.arange(block_order.shape[0], dtype=jnp.int32)
    matches = block_index[:, None] == block_ids[None, :]
    start = jnp.sum(jnp.where(matches, block_order[None, :], 0), axis=1)
    return start * BLK + token_index % BLK


def _nt(a, b):
    return lax.dot_general(a, b, (((1,), (1,)), ((), ())), preferred_element_type=jnp.float32)


def _tn(a, b):
    return lax.dot_general(a, b, (((0,), (0,)), ((), ())), preferred_element_type=jnp.float32)


def stats_call(pair_all, kv_all, qpos, kpos, scaling):
    q_total = pair_all.shape[0]
    n = kv_all.shape[0]

    def kernel(q_ref, g_ref, k_ref, v_ref, qp_ref, kp_ref, m_ref, l_ref, w_ref):
        s = _nt(k_ref[...], q_ref[...]) * scaling
        vis = kp_ref[...] <= qp_ref[...]
        s = jnp.where(vis, s, -1e30)
        m = jnp.max(s, axis=0, keepdims=True)
        e = jnp.exp(s - jnp.maximum(m, -1e29))
        dp = _nt(v_ref[...], g_ref[...])
        m_ref[...] = m
        l_ref[...] = jnp.sum(e, axis=0, keepdims=True)
        w_ref[...] = jnp.sum(e * dp, axis=0, keepdims=True)

    stat_blk = pl.BlockSpec((None, 1, TQ), lambda b, h: (h, 0, b))
    out = jax.ShapeDtypeStruct((H, 1, q_total), jnp.float32)
    return pl.pallas_call(
        kernel,
        grid=(q_total // TQ, H),
        in_specs=[
            pl.BlockSpec((TQ, HD), lambda b, h: (b, h)),
            pl.BlockSpec((TQ, HD), lambda b, h: (b, H + h)),
            pl.BlockSpec((n, HD), lambda b, h: (0, 0)),
            pl.BlockSpec((n, HD), lambda b, h: (0, 1)),
            pl.BlockSpec((1, TQ), lambda b, h: (0, b)),
            pl.BlockSpec((n, 1), lambda b, h: (0, 0)),
        ],
        out_specs=[stat_blk, stat_blk, stat_blk],
        out_shape=[out, out, out],
        compiler_params=pltpu.CompilerParams(dimension_semantics=("arbitrary", "arbitrary")),
        interpret=INTERPRET,
    )(pair_all, pair_all, kv_all, kv_all, qpos, kpos)


def grad_call(pair_all, kv_all, qpos, kpos, logsum, deltas, scaling):
    q_total = pair_all.shape[0]
    n = kv_all.shape[0]

    def kernel(q_ref, g_ref, k_ref, v_ref, qp_ref, kp_ref, ls_ref, dl_ref, dq_ref, kv_ref):
        first = (pl.program_id(0) == 0) & (pl.program_id(1) == 0)
        q = q_ref[...]
        g = g_ref[...]
        k = k_ref[...]
        s = _nt(k, q) * scaling
        vis = kp_ref[...] <= qp_ref[...]
        p = jnp.exp(jnp.where(vis, s, -1e30) - ls_ref[...])
        dp = _nt(v_ref[...], g)
        ds = (p * (dp - dl_ref[...])).astype(jnp.bfloat16)
        pb = p.astype(jnp.bfloat16)
        dq_ref[...] = _tn(ds, k)

        @pl.when(first)
        def _():
            kv_ref[...] = jnp.zeros_like(kv_ref)

        kv_ref[:, :HD] += jnp.dot(ds, q, preferred_element_type=jnp.float32)
        kv_ref[:, HD:] += jnp.dot(pb, g, preferred_element_type=jnp.float32)

    stat_blk = pl.BlockSpec((None, 1, TQ), lambda b, h: (h, 0, b))
    return pl.pallas_call(
        kernel,
        grid=(q_total // TQ, H),
        in_specs=[
            pl.BlockSpec((TQ, HD), lambda b, h: (b, h)),
            pl.BlockSpec((TQ, HD), lambda b, h: (b, H + h)),
            pl.BlockSpec((n, HD), lambda b, h: (0, 0)),
            pl.BlockSpec((n, HD), lambda b, h: (0, 1)),
            pl.BlockSpec((1, TQ), lambda b, h: (0, b)),
            pl.BlockSpec((n, 1), lambda b, h: (0, 0)),
            stat_blk,
            stat_blk,
        ],
        out_specs=[
            pl.BlockSpec((TQ, HD), lambda b, h: (b, h)),
            pl.BlockSpec((n, 2 * HD), lambda b, h: (0, 0)),
        ],
        out_shape=[
            jax.ShapeDtypeStruct((q_total, H * HD), jnp.float32),
            jax.ShapeDtypeStruct((n, 2 * HD), jnp.float32),
        ],
        compiler_params=pltpu.CompilerParams(dimension_semantics=("arbitrary", "arbitrary")),
        interpret=INTERPRET,
    )(pair_all, pair_all, kv_all, kv_all, qpos, kpos, logsum, deltas)


def tile_grid(queries, key_states, value_states, out_grad, block_order, scaling):
    row_amount = lax.axis_size("row")
    col_amount = lax.axis_size("col")
    r = lax.axis_index("row")
    c = lax.axis_index("col")
    local_rows = queries.shape[0]
    pair = jnp.concatenate([queries, out_grad], axis=1)
    pair_all = lax.all_to_all(jnp.tile(pair, (row_amount, 1)), "row", 0, 0, tiled=True)
    kv_all = lax.all_gather(
        jnp.concatenate([key_states, value_states], axis=1), "col", axis=0, tiled=True
    )
    q_total = pair_all.shape[0]
    k_total = kv_all.shape[0]

    qi = jnp.arange(q_total, dtype=jnp.int32)
    q_anchor = ((qi // local_rows) * col_amount + c) * local_rows + qi % local_rows
    qpos = positions(q_anchor, block_order).reshape(1, q_total)
    ki = jnp.arange(k_total, dtype=jnp.int32)
    k_anchor = ((ki // local_rows) * row_amount + r) * local_rows + ki % local_rows
    kpos = positions(k_anchor, block_order).reshape(k_total, 1)

    maxima, summed, weighted = stats_call(pair_all, kv_all, qpos, kpos, scaling)
    stacked = jnp.stack([maxima[:, 0], summed[:, 0], weighted[:, 0]])
    gathered = lax.all_gather(stacked, "row", axis=0, tiled=True)
    gathered = gathered.reshape(row_amount, 3, H, q_total)
    top = jnp.max(gathered[:, 0], axis=0)
    factor = jnp.exp(gathered[:, 0] - top[None])
    summed = jnp.sum(gathered[:, 1] * factor, axis=0)
    weighted = jnp.sum(gathered[:, 2] * factor, axis=0)
    logsum = (top + jnp.log(summed)).reshape(H, 1, q_total)
    deltas = (weighted / summed).reshape(H, 1, q_total)

    query_acc, kv_parts = grad_call(pair_all, kv_all, qpos, kpos, logsum, deltas, scaling)
    kv_grad = lax.psum_scatter(kv_parts, "col", scatter_dimension=0, tiled=True)
    key_grad, value_grad = kv_grad[:, :HD], kv_grad[:, HD:]
    exchanged = lax.all_to_all(query_acc, "row", 0, 0, tiled=True)
    query_grad = jnp.sum(exchanged.reshape(row_amount, local_rows, H * HD), axis=0)
    return (
        (query_grad * scaling).astype(jnp.bfloat16),
        (key_grad * scaling).astype(jnp.bfloat16),
        value_grad.astype(jnp.bfloat16),
    )


def local(queries, key_states, value_states, out_grad, block_order):
    scaling = 1.0 / math.sqrt(key_states.shape[1])
    return tile_grid(queries, key_states, value_states, out_grad, block_order, scaling)


def solution(mesh):
    placed = (
        P(("row", "col"), None),
        P(("col", "row"), None),
        P(("col", "row"), None),
        P(("row", "col"), None),
        P(),
    )
    return jax.shard_map(
        local,
        mesh=mesh,
        in_specs=placed,
        out_specs=(P(("row", "col"), None), P(("col", "row"), None), P(("col", "row"), None)),
        check_vma=False,
    )
```

```python
import math
import os

import jax
import jax.numpy as jnp
from jax import lax
from jax.experimental import pallas as pl
from jax.experimental.pallas import tpu as pltpu
from jax.sharding import PartitionSpec as P

H = 8
HD = 128
BLK = 64
TQ = 256
INTERPRET = bool(os.environ.get("SOL_INTERPRET"))


def positions(token_index, block_order):
    block_index = token_index // BLK
    block_ids = jnp.arange(block_order.shape[0], dtype=jnp.int32)
    matches = block_index[:, None] == block_ids[None, :]
    start = jnp.sum(jnp.where(matches, block_order[None, :], 0), axis=1)
    return start * BLK + token_index % BLK


def _nt(a, b):
    return lax.dot_general(a, b, (((1,), (1,)), ((), ())), preferred_element_type=jnp.float32)


def _tn(a, b):
    return lax.dot_general(a, b, (((0,), (0,)), ((), ())), preferred_element_type=jnp.float32)


def stats_call(pair_all, kv_all, qpos, kpos, scaling):
    q_total = pair_all.shape[0]
    n = kv_all.shape[0]

    def kernel(q_ref, g_ref, k_ref, v_ref, qp_ref, kp_ref, m_ref, l_ref, w_ref):
        s = _nt(k_ref[...], q_ref[...]) * scaling
        vis = kp_ref[...] <= qp_ref[...]
        s = jnp.where(vis, s, -1e30)
        m = jnp.max(s, axis=0, keepdims=True)
        e = jnp.exp(s - jnp.maximum(m, -1e29))
        dp = _nt(v_ref[...], g_ref[...])
        m_ref[...] = m
        l_ref[...] = jnp.sum(e, axis=0, keepdims=True)
        w_ref[...] = jnp.sum(e * dp, axis=0, keepdims=True)

    stat_blk = pl.BlockSpec((None, 1, TQ), lambda b, h: (h, 0, b))
    out = jax.ShapeDtypeStruct((H, 1, q_total), jnp.float32)
    return pl.pallas_call(
        kernel,
        grid=(q_total // TQ, H),
        in_specs=[
            pl.BlockSpec((TQ, HD), lambda b, h: (b, h)),
            pl.BlockSpec((TQ, HD), lambda b, h: (b, H + h)),
            pl.BlockSpec((n, HD), lambda b, h: (0, 0)),
            pl.BlockSpec((n, HD), lambda b, h: (0, 1)),
            pl.BlockSpec((1, TQ), lambda b, h: (0, b)),
            pl.BlockSpec((n, 1), lambda b, h: (0, 0)),
        ],
        out_specs=[stat_blk, stat_blk, stat_blk],
        out_shape=[out, out, out],
        compiler_params=pltpu.CompilerParams(dimension_semantics=("arbitrary", "arbitrary")),
        interpret=INTERPRET,
    )(pair_all, pair_all, kv_all, kv_all, qpos, kpos)


def grad_call(pair_all, kv_all, qpos, kpos, logsum, deltas, scaling):
    q_total = pair_all.shape[0]
    n = kv_all.shape[0]

    def kernel(q_ref, g_ref, k_ref, v_ref, qp_ref, kp_ref, ls_ref, dl_ref, dq_ref, kv_ref):
        first = (pl.program_id(0) == 0) & (pl.program_id(1) == 0)
        q = q_ref[...]
        g = g_ref[...]
        k = k_ref[...]
        s = _nt(k, q) * scaling
        vis = kp_ref[...] <= qp_ref[...]
        p = jnp.exp(jnp.where(vis, s, -1e30) - ls_ref[...])
        dp = _nt(v_ref[...], g)
        ds = (p * (dp - dl_ref[...])).astype(jnp.bfloat16)
        pb = p.astype(jnp.bfloat16)
        dq_ref[...] = _tn(ds, k)

        @pl.when(first)
        def _():
            kv_ref[...] = jnp.zeros_like(kv_ref)

        kv_ref[:, :HD] += jnp.dot(ds, q, preferred_element_type=jnp.float32)
        kv_ref[:, HD:] += jnp.dot(pb, g, preferred_element_type=jnp.float32)

    stat_blk = pl.BlockSpec((None, 1, TQ), lambda b, h: (h, 0, b))
    return pl.pallas_call(
        kernel,
        grid=(q_total // TQ, H),
        in_specs=[
            pl.BlockSpec((TQ, HD), lambda b, h: (b, h)),
            pl.BlockSpec((TQ, HD), lambda b, h: (b, H + h)),
            pl.BlockSpec((n, HD), lambda b, h: (0, 0)),
            pl.BlockSpec((n, HD), lambda b, h: (0, 1)),
            pl.BlockSpec((1, TQ), lambda b, h: (0, b)),
            pl.BlockSpec((n, 1), lambda b, h: (0, 0)),
            stat_blk,
            stat_blk,
        ],
        out_specs=[
            pl.BlockSpec((TQ, HD), lambda b, h: (b, h)),
            pl.BlockSpec((n, 2 * HD), lambda b, h: (0, 0)),
        ],
        out_shape=[
            jax.ShapeDtypeStruct((q_total, H * HD), jnp.float32),
            jax.ShapeDtypeStruct((n, 2 * HD), jnp.float32),
        ],
        compiler_params=pltpu.CompilerParams(dimension_semantics=("arbitrary", "arbitrary")),
        interpret=INTERPRET,
    )(pair_all, pair_all, kv_all, kv_all, qpos, kpos, logsum, deltas)


def tile_grid(queries, key_states, value_states, out_grad, block_order, scaling):
    row_amount = lax.axis_size("row")
    col_amount = lax.axis_size("col")
    r = lax.axis_index("row")
    c = lax.axis_index("col")
    local_rows = queries.shape[0]
    pair = jnp.concatenate([queries, out_grad], axis=1)
    pair_all = lax.all_to_all(jnp.tile(pair, (row_amount, 1)), "row", 0, 0, tiled=True)
    kv_all = lax.all_gather(
        jnp.concatenate([key_states, value_states], axis=1), "col", axis=0, tiled=True
    )
    q_total = pair_all.shape[0]
    k_total = kv_all.shape[0]

    qi = jnp.arange(q_total, dtype=jnp.int32)
    q_anchor = ((qi // local_rows) * col_amount + c) * local_rows + qi % local_rows
    qpos = positions(q_anchor, block_order).reshape(1, q_total)
    ki = jnp.arange(k_total, dtype=jnp.int32)
    k_anchor = ((ki // local_rows) * row_amount + r) * local_rows + ki % local_rows
    kpos = positions(k_anchor, block_order).reshape(k_total, 1)

    maxima, summed, weighted = stats_call(pair_all, kv_all, qpos, kpos, scaling)
    stacked = jnp.stack([maxima[:, 0], summed[:, 0], weighted[:, 0]])
    gathered = lax.all_to_all(
        jnp.tile(stacked[None], (row_amount, 1, 1, 1)), "row", 0, 0, tiled=True
    )
    top = jnp.max(gathered[:, 0], axis=0)
    factor = jnp.exp(gathered[:, 0] - top[None])
    summed = jnp.sum(gathered[:, 1] * factor, axis=0)
    weighted = jnp.sum(gathered[:, 2] * factor, axis=0)
    logsum = (top + jnp.log(summed)).reshape(H, 1, q_total)
    deltas = (weighted / summed).reshape(H, 1, q_total)

    query_acc, kv_parts = grad_call(pair_all, kv_all, qpos, kpos, logsum, deltas, scaling)
    kv_grad = lax.psum_scatter(kv_parts, "col", scatter_dimension=0, tiled=True)
    key_grad, value_grad = kv_grad[:, :HD], kv_grad[:, HD:]
    exchanged = lax.all_to_all(query_acc, "row", 0, 0, tiled=True)
    query_grad = jnp.sum(exchanged.reshape(row_amount, local_rows, H * HD), axis=0)
    return (
        (query_grad * scaling).astype(jnp.bfloat16),
        (key_grad * scaling).astype(jnp.bfloat16),
        value_grad.astype(jnp.bfloat16),
    )


def local(queries, key_states, value_states, out_grad, block_order):
    scaling = 1.0 / math.sqrt(key_states.shape[1])
    return tile_grid(queries, key_states, value_states, out_grad, block_order, scaling)


def solution(mesh):
    placed = (
        P(("row", "col"), None),
        P(("col", "row"), None),
        P(("col", "row"), None),
        P(("row", "col"), None),
        P(),
    )
    return jax.shard_map(
        local,
        mesh=mesh,
        in_specs=placed,
        out_specs=(P(("row", "col"), None), P(("col", "row"), None), P(("col", "row"), None)),
        check_vma=False,
    )
```

```python
import math
import os

import jax
import jax.numpy as jnp
from jax import lax
from jax.experimental import pallas as pl
from jax.experimental.pallas import tpu as pltpu
from jax.sharding import PartitionSpec as P

H = 8
HD = 128
BLK = 64
TQ = 512
INTERPRET = bool(os.environ.get("SOL_INTERPRET"))


def positions(token_index, block_order):
    block_index = token_index // BLK
    block_ids = jnp.arange(block_order.shape[0], dtype=jnp.int32)
    matches = block_index[:, None] == block_ids[None, :]
    start = jnp.sum(jnp.where(matches, block_order[None, :], 0), axis=1)
    return start * BLK + token_index % BLK


def _nt(a, b):
    return lax.dot_general(a, b, (((1,), (1,)), ((), ())), preferred_element_type=jnp.float32)


def _tn(a, b):
    return lax.dot_general(a, b, (((0,), (0,)), ((), ())), preferred_element_type=jnp.float32)


def stats_call(pair_all, kv_all, qpos, kpos, scaling):
    q_total = pair_all.shape[0]
    n = kv_all.shape[0]

    def kernel(q_ref, g_ref, k_ref, v_ref, qp_ref, kp_ref, m_ref, l_ref, w_ref):
        s = _nt(k_ref[...], q_ref[...]) * scaling
        vis = kp_ref[...] <= qp_ref[...]
        s = jnp.where(vis, s, -1e30)
        m = jnp.max(s, axis=0, keepdims=True)
        e = jnp.exp(s - jnp.maximum(m, -1e29))
        dp = _nt(v_ref[...], g_ref[...])
        m_ref[...] = m
        l_ref[...] = jnp.sum(e, axis=0, keepdims=True)
        w_ref[...] = jnp.sum(e * dp, axis=0, keepdims=True)

    stat_blk = pl.BlockSpec((None, 1, TQ), lambda b, h: (h, 0, b))
    out = jax.ShapeDtypeStruct((H, 1, q_total), jnp.float32)
    return pl.pallas_call(
        kernel,
        grid=(q_total // TQ, H),
        in_specs=[
            pl.BlockSpec((TQ, HD), lambda b, h: (b, h)),
            pl.BlockSpec((TQ, HD), lambda b, h: (b, H + h)),
            pl.BlockSpec((n, HD), lambda b, h: (0, 0)),
            pl.BlockSpec((n, HD), lambda b, h: (0, 1)),
            pl.BlockSpec((1, TQ), lambda b, h: (0, b)),
            pl.BlockSpec((n, 1), lambda b, h: (0, 0)),
        ],
        out_specs=[stat_blk, stat_blk, stat_blk],
        out_shape=[out, out, out],
        compiler_params=pltpu.CompilerParams(dimension_semantics=("arbitrary", "arbitrary")),
        interpret=INTERPRET,
    )(pair_all, pair_all, kv_all, kv_all, qpos, kpos)


def grad_call(pair_all, kv_all, qpos, kpos, logsum, deltas, scaling):
    q_total = pair_all.shape[0]
    n = kv_all.shape[0]

    def kernel(q_ref, g_ref, k_ref, v_ref, qp_ref, kp_ref, ls_ref, dl_ref, dq_ref, kv_ref):
        first = (pl.program_id(0) == 0) & (pl.program_id(1) == 0)
        q = q_ref[...]
        g = g_ref[...]
        k = k_ref[...]
        s = _nt(k, q) * scaling
        vis = kp_ref[...] <= qp_ref[...]
        p = jnp.exp(jnp.where(vis, s, -1e30) - ls_ref[...])
        dp = _nt(v_ref[...], g)
        ds = (p * (dp - dl_ref[...])).astype(jnp.bfloat16)
        pb = p.astype(jnp.bfloat16)
        dq_ref[...] = _tn(ds, k)

        @pl.when(first)
        def _():
            kv_ref[...] = jnp.zeros_like(kv_ref)

        kv_ref[:, :HD] += jnp.dot(ds, q, preferred_element_type=jnp.float32)
        kv_ref[:, HD:] += jnp.dot(pb, g, preferred_element_type=jnp.float32)

    stat_blk = pl.BlockSpec((None, 1, TQ), lambda b, h: (h, 0, b))
    return pl.pallas_call(
        kernel,
        grid=(q_total // TQ, H),
        in_specs=[
            pl.BlockSpec((TQ, HD), lambda b, h: (b, h)),
            pl.BlockSpec((TQ, HD), lambda b, h: (b, H + h)),
            pl.BlockSpec((n, HD), lambda b, h: (0, 0)),
            pl.BlockSpec((n, HD), lambda b, h: (0, 1)),
            pl.BlockSpec((1, TQ), lambda b, h: (0, b)),
            pl.BlockSpec((n, 1), lambda b, h: (0, 0)),
            stat_blk,
            stat_blk,
        ],
        out_specs=[
            pl.BlockSpec((TQ, HD), lambda b, h: (b, h)),
            pl.BlockSpec((n, 2 * HD), lambda b, h: (0, 0)),
        ],
        out_shape=[
            jax.ShapeDtypeStruct((q_total, H * HD), jnp.float32),
            jax.ShapeDtypeStruct((n, 2 * HD), jnp.float32),
        ],
        compiler_params=pltpu.CompilerParams(dimension_semantics=("arbitrary", "arbitrary")),
        interpret=INTERPRET,
    )(pair_all, pair_all, kv_all, kv_all, qpos, kpos, logsum, deltas)


def tile_grid(queries, key_states, value_states, out_grad, block_order, scaling):
    row_amount = lax.axis_size("row")
    col_amount = lax.axis_size("col")
    r = lax.axis_index("row")
    c = lax.axis_index("col")
    local_rows = queries.shape[0]
    pair = jnp.concatenate([queries, out_grad], axis=1)
    pair_all = lax.all_to_all(jnp.tile(pair, (row_amount, 1)), "row", 0, 0, tiled=True)
    kv_all = lax.all_gather(
        jnp.concatenate([key_states, value_states], axis=1), "col", axis=0, tiled=True
    )
    q_total = pair_all.shape[0]
    k_total = kv_all.shape[0]

    qi = jnp.arange(q_total, dtype=jnp.int32)
    q_anchor = ((qi // local_rows) * col_amount + c) * local_rows + qi % local_rows
    qpos = positions(q_anchor, block_order).reshape(1, q_total)
    ki = jnp.arange(k_total, dtype=jnp.int32)
    k_anchor = ((ki // local_rows) * row_amount + r) * local_rows + ki % local_rows
    kpos = positions(k_anchor, block_order).reshape(k_total, 1)

    maxima, summed, weighted = stats_call(pair_all, kv_all, qpos, kpos, scaling)
    stacked = jnp.stack([maxima[:, 0], summed[:, 0], weighted[:, 0]])
    gathered = lax.all_to_all(
        jnp.tile(stacked[None], (row_amount, 1, 1, 1)), "row", 0, 0, tiled=True
    )
    top = jnp.max(gathered[:, 0], axis=0)
    factor = jnp.exp(gathered[:, 0] - top[None])
    summed = jnp.sum(gathered[:, 1] * factor, axis=0)
    weighted = jnp.sum(gathered[:, 2] * factor, axis=0)
    logsum = (top + jnp.log(summed)).reshape(H, 1, q_total)
    deltas = (weighted / summed).reshape(H, 1, q_total)

    query_acc, kv_parts = grad_call(pair_all, kv_all, qpos, kpos, logsum, deltas, scaling)
    kv_grad = lax.psum_scatter(kv_parts, "col", scatter_dimension=0, tiled=True)
    key_grad, value_grad = kv_grad[:, :HD], kv_grad[:, HD:]
    exchanged = lax.all_to_all(query_acc, "row", 0, 0, tiled=True)
    query_grad = jnp.sum(exchanged.reshape(row_amount, local_rows, H * HD), axis=0)
    return (
        (query_grad * scaling).astype(jnp.bfloat16),
        (key_grad * scaling).astype(jnp.bfloat16),
        value_grad.astype(jnp.bfloat16),
    )


def local(queries, key_states, value_states, out_grad, block_order):
    scaling = 1.0 / math.sqrt(key_states.shape[1])
    return tile_grid(queries, key_states, value_states, out_grad, block_order, scaling)


def solution(mesh):
    placed = (
        P(("row", "col"), None),
        P(("col", "row"), None),
        P(("col", "row"), None),
        P(("row", "col"), None),
        P(),
    )
    return jax.shard_map(
        local,
        mesh=mesh,
        in_specs=placed,
        out_specs=(P(("row", "col"), None), P(("col", "row"), None), P(("col", "row"), None)),
        check_vma=False,
    )
```

```python
import math
import os

import jax
import jax.numpy as jnp
from jax import lax
from jax.experimental import pallas as pl
from jax.experimental.pallas import tpu as pltpu
from jax.sharding import PartitionSpec as P

H = 8
HD = 128
BLK = 64
TQ = 256
TS = 512
INTERPRET = bool(os.environ.get("SOL_INTERPRET"))


def positions(token_index, block_order):
    block_index = token_index // BLK
    block_ids = jnp.arange(block_order.shape[0], dtype=jnp.int32)
    matches = block_index[:, None] == block_ids[None, :]
    start = jnp.sum(jnp.where(matches, block_order[None, :], 0), axis=1)
    return start * BLK + token_index % BLK


def _nt(a, b):
    return lax.dot_general(a, b, (((1,), (1,)), ((), ())), preferred_element_type=jnp.float32)


def _tn(a, b):
    return lax.dot_general(a, b, (((0,), (0,)), ((), ())), preferred_element_type=jnp.float32)


def stats_call(pair_all, kv_all, qpos, kpos, scaling):
    q_total = pair_all.shape[0]
    n = kv_all.shape[0]

    def kernel(q_ref, g_ref, k_ref, v_ref, qp_ref, kp_ref, m_ref, l_ref, w_ref):
        s = _nt(k_ref[...], q_ref[...]) * scaling
        vis = kp_ref[...] <= qp_ref[...]
        s = jnp.where(vis, s, -1e30)
        m = jnp.max(s, axis=0, keepdims=True)
        e = jnp.exp(s - jnp.maximum(m, -1e29))
        dp = _nt(v_ref[...], g_ref[...])
        m_ref[...] = m
        l_ref[...] = jnp.sum(e, axis=0, keepdims=True)
        w_ref[...] = jnp.sum(e * dp, axis=0, keepdims=True)

    stat_blk = pl.BlockSpec((None, 1, TS), lambda b, h: (h, 0, b))
    out = jax.ShapeDtypeStruct((H, 1, q_total), jnp.float32)
    return pl.pallas_call(
        kernel,
        grid=(q_total // TS, H),
        in_specs=[
            pl.BlockSpec((TS, HD), lambda b, h: (b, h)),
            pl.BlockSpec((TS, HD), lambda b, h: (b, H + h)),
            pl.BlockSpec((n, HD), lambda b, h: (0, 0)),
            pl.BlockSpec((n, HD), lambda b, h: (0, 1)),
            pl.BlockSpec((1, TS), lambda b, h: (0, b)),
            pl.BlockSpec((n, 1), lambda b, h: (0, 0)),
        ],
        out_specs=[stat_blk, stat_blk, stat_blk],
        out_shape=[out, out, out],
        compiler_params=pltpu.CompilerParams(dimension_semantics=("arbitrary", "arbitrary")),
        interpret=INTERPRET,
    )(pair_all, pair_all, kv_all, kv_all, qpos, kpos)


def grad_call(pair_all, kv_all, qpos, kpos, logsum, deltas, scaling):
    q_total = pair_all.shape[0]
    n = kv_all.shape[0]

    def kernel(q_ref, g_ref, k_ref, v_ref, qp_ref, kp_ref, ls_ref, dl_ref, dq_ref, kv_ref):
        first = (pl.program_id(0) == 0) & (pl.program_id(1) == 0)
        q = q_ref[...]
        g = g_ref[...]
        k = k_ref[...]
        s = _nt(k, q) * scaling
        vis = kp_ref[...] <= qp_ref[...]
        p = jnp.exp(jnp.where(vis, s, -1e30) - ls_ref[...])
        dp = _nt(v_ref[...], g)
        ds = (p * (dp - dl_ref[...])).astype(jnp.bfloat16)
        pb = p.astype(jnp.bfloat16)
        dq_ref[...] = _tn(ds, k)

        @pl.when(first)
        def _():
            kv_ref[...] = jnp.zeros_like(kv_ref)

        kv_ref[:, :HD] += jnp.dot(ds, q, preferred_element_type=jnp.float32)
        kv_ref[:, HD:] += jnp.dot(pb, g, preferred_element_type=jnp.float32)

    stat_blk = pl.BlockSpec((None, 1, TQ), lambda b, h: (h, 0, b))
    return pl.pallas_call(
        kernel,
        grid=(q_total // TQ, H),
        in_specs=[
            pl.BlockSpec((TQ, HD), lambda b, h: (b, h)),
            pl.BlockSpec((TQ, HD), lambda b, h: (b, H + h)),
            pl.BlockSpec((n, HD), lambda b, h: (0, 0)),
            pl.BlockSpec((n, HD), lambda b, h: (0, 1)),
            pl.BlockSpec((1, TQ), lambda b, h: (0, b)),
            pl.BlockSpec((n, 1), lambda b, h: (0, 0)),
            stat_blk,
            stat_blk,
        ],
        out_specs=[
            pl.BlockSpec((TQ, HD), lambda b, h: (b, h)),
            pl.BlockSpec((n, 2 * HD), lambda b, h: (0, 0)),
        ],
        out_shape=[
            jax.ShapeDtypeStruct((q_total, H * HD), jnp.float32),
            jax.ShapeDtypeStruct((n, 2 * HD), jnp.float32),
        ],
        compiler_params=pltpu.CompilerParams(dimension_semantics=("arbitrary", "arbitrary")),
        interpret=INTERPRET,
    )(pair_all, pair_all, kv_all, kv_all, qpos, kpos, logsum, deltas)


def tile_grid(queries, key_states, value_states, out_grad, block_order, scaling):
    row_amount = lax.axis_size("row")
    col_amount = lax.axis_size("col")
    r = lax.axis_index("row")
    c = lax.axis_index("col")
    local_rows = queries.shape[0]
    pair = jnp.concatenate([queries, out_grad], axis=1)
    pair_all = lax.all_to_all(jnp.tile(pair, (row_amount, 1)), "row", 0, 0, tiled=True)
    kv_all = lax.all_gather(
        jnp.concatenate([key_states, value_states], axis=1), "col", axis=0, tiled=True
    )
    q_total = pair_all.shape[0]
    k_total = kv_all.shape[0]

    qi = jnp.arange(q_total, dtype=jnp.int32)
    q_anchor = ((qi // local_rows) * col_amount + c) * local_rows + qi % local_rows
    qpos = positions(q_anchor, block_order).reshape(1, q_total)
    ki = jnp.arange(k_total, dtype=jnp.int32)
    k_anchor = ((ki // local_rows) * row_amount + r) * local_rows + ki % local_rows
    kpos = positions(k_anchor, block_order).reshape(k_total, 1)

    maxima, summed, weighted = stats_call(pair_all, kv_all, qpos, kpos, scaling)
    stacked = jnp.stack([maxima[:, 0], summed[:, 0], weighted[:, 0]])
    gathered = lax.all_to_all(
        jnp.tile(stacked[None], (row_amount, 1, 1, 1)), "row", 0, 0, tiled=True
    )
    top = jnp.max(gathered[:, 0], axis=0)
    factor = jnp.exp(gathered[:, 0] - top[None])
    summed = jnp.sum(gathered[:, 1] * factor, axis=0)
    weighted = jnp.sum(gathered[:, 2] * factor, axis=0)
    logsum = (top + jnp.log(summed)).reshape(H, 1, q_total)
    deltas = (weighted / summed).reshape(H, 1, q_total)

    query_acc, kv_parts = grad_call(pair_all, kv_all, qpos, kpos, logsum, deltas, scaling)
    kv_grad = lax.psum_scatter(kv_parts, "col", scatter_dimension=0, tiled=True)
    key_grad, value_grad = kv_grad[:, :HD], kv_grad[:, HD:]
    exchanged = lax.all_to_all(query_acc, "row", 0, 0, tiled=True)
    query_grad = jnp.sum(exchanged.reshape(row_amount, local_rows, H * HD), axis=0)
    return (
        (query_grad * scaling).astype(jnp.bfloat16),
        (key_grad * scaling).astype(jnp.bfloat16),
        value_grad.astype(jnp.bfloat16),
    )


def local(queries, key_states, value_states, out_grad, block_order):
    scaling = 1.0 / math.sqrt(key_states.shape[1])
    return tile_grid(queries, key_states, value_states, out_grad, block_order, scaling)


def solution(mesh):
    placed = (
        P(("row", "col"), None),
        P(("col", "row"), None),
        P(("col", "row"), None),
        P(("row", "col"), None),
        P(),
    )
    return jax.shard_map(
        local,
        mesh=mesh,
        in_specs=placed,
        out_specs=(P(("row", "col"), None), P(("col", "row"), None), P(("col", "row"), None)),
        check_vma=False,
    )
```

```python
import math
import os

import jax
import jax.numpy as jnp
from jax import lax
from jax.experimental import pallas as pl
from jax.experimental.pallas import tpu as pltpu
from jax.sharding import PartitionSpec as P

H = 8
HD = 128
BLK = 64
TQ = 128
TS = 1024
INTERPRET = bool(os.environ.get("SOL_INTERPRET"))


def positions(token_index, block_order):
    block_index = token_index // BLK
    block_ids = jnp.arange(block_order.shape[0], dtype=jnp.int32)
    matches = block_index[:, None] == block_ids[None, :]
    start = jnp.sum(jnp.where(matches, block_order[None, :], 0), axis=1)
    return start * BLK + token_index % BLK


def _nt(a, b):
    return lax.dot_general(a, b, (((1,), (1,)), ((), ())), preferred_element_type=jnp.float32)


def _tn(a, b):
    return lax.dot_general(a, b, (((0,), (0,)), ((), ())), preferred_element_type=jnp.float32)


def stats_call(pair_all, kv_all, qpos, kpos, scaling):
    q_total = pair_all.shape[0]
    n = kv_all.shape[0]

    def kernel(q_ref, g_ref, k_ref, v_ref, qp_ref, kp_ref, m_ref, l_ref, w_ref):
        s = _nt(k_ref[...], q_ref[...]) * scaling
        vis = kp_ref[...] <= qp_ref[...]
        s = jnp.where(vis, s, -1e30)
        m = jnp.max(s, axis=0, keepdims=True)
        e = jnp.exp(s - jnp.maximum(m, -1e29))
        dp = _nt(v_ref[...], g_ref[...])
        m_ref[...] = m
        l_ref[...] = jnp.sum(e, axis=0, keepdims=True)
        w_ref[...] = jnp.sum(e * dp, axis=0, keepdims=True)

    stat_blk = pl.BlockSpec((None, 1, TS), lambda b, h: (h, 0, b))
    out = jax.ShapeDtypeStruct((H, 1, q_total), jnp.float32)
    return pl.pallas_call(
        kernel,
        grid=(q_total // TS, H),
        in_specs=[
            pl.BlockSpec((TS, HD), lambda b, h: (b, h)),
            pl.BlockSpec((TS, HD), lambda b, h: (b, H + h)),
            pl.BlockSpec((n, HD), lambda b, h: (0, 0)),
            pl.BlockSpec((n, HD), lambda b, h: (0, 1)),
            pl.BlockSpec((1, TS), lambda b, h: (0, b)),
            pl.BlockSpec((n, 1), lambda b, h: (0, 0)),
        ],
        out_specs=[stat_blk, stat_blk, stat_blk],
        out_shape=[out, out, out],
        compiler_params=pltpu.CompilerParams(dimension_semantics=("arbitrary", "arbitrary")),
        interpret=INTERPRET,
    )(pair_all, pair_all, kv_all, kv_all, qpos, kpos)


def grad_call(pair_all, kv_all, qpos, kpos, logsum, deltas, scaling):
    q_total = pair_all.shape[0]
    n = kv_all.shape[0]

    def kernel(q_ref, g_ref, k_ref, v_ref, qp_ref, kp_ref, ls_ref, dl_ref, dq_ref, kv_ref):
        first = (pl.program_id(0) == 0) & (pl.program_id(1) == 0)
        q = q_ref[...]
        g = g_ref[...]
        k = k_ref[...]
        s = _nt(k, q) * scaling
        vis = kp_ref[...] <= qp_ref[...]
        p = jnp.exp(jnp.where(vis, s, -1e30) - ls_ref[...])
        dp = _nt(v_ref[...], g)
        ds = (p * (dp - dl_ref[...])).astype(jnp.bfloat16)
        pb = p.astype(jnp.bfloat16)
        dq_ref[...] = _tn(ds, k)

        @pl.when(first)
        def _():
            kv_ref[...] = jnp.zeros_like(kv_ref)

        kv_ref[:, :HD] += jnp.dot(ds, q, preferred_element_type=jnp.float32)
        kv_ref[:, HD:] += jnp.dot(pb, g, preferred_element_type=jnp.float32)

    stat_blk = pl.BlockSpec((None, 1, TQ), lambda b, h: (h, 0, b))
    return pl.pallas_call(
        kernel,
        grid=(q_total // TQ, H),
        in_specs=[
            pl.BlockSpec((TQ, HD), lambda b, h: (b, h)),
            pl.BlockSpec((TQ, HD), lambda b, h: (b, H + h)),
            pl.BlockSpec((n, HD), lambda b, h: (0, 0)),
            pl.BlockSpec((n, HD), lambda b, h: (0, 1)),
            pl.BlockSpec((1, TQ), lambda b, h: (0, b)),
            pl.BlockSpec((n, 1), lambda b, h: (0, 0)),
            stat_blk,
            stat_blk,
        ],
        out_specs=[
            pl.BlockSpec((TQ, HD), lambda b, h: (b, h)),
            pl.BlockSpec((n, 2 * HD), lambda b, h: (0, 0)),
        ],
        out_shape=[
            jax.ShapeDtypeStruct((q_total, H * HD), jnp.float32),
            jax.ShapeDtypeStruct((n, 2 * HD), jnp.float32),
        ],
        compiler_params=pltpu.CompilerParams(dimension_semantics=("arbitrary", "arbitrary")),
        interpret=INTERPRET,
    )(pair_all, pair_all, kv_all, kv_all, qpos, kpos, logsum, deltas)


def tile_grid(queries, key_states, value_states, out_grad, block_order, scaling):
    row_amount = lax.axis_size("row")
    col_amount = lax.axis_size("col")
    r = lax.axis_index("row")
    c = lax.axis_index("col")
    local_rows = queries.shape[0]
    pair = jnp.concatenate([queries, out_grad], axis=1)
    pair_all = lax.all_to_all(jnp.tile(pair, (row_amount, 1)), "row", 0, 0, tiled=True)
    kv_all = lax.all_gather(
        jnp.concatenate([key_states, value_states], axis=1), "col", axis=0, tiled=True
    )
    q_total = pair_all.shape[0]
    k_total = kv_all.shape[0]

    qi = jnp.arange(q_total, dtype=jnp.int32)
    q_anchor = ((qi // local_rows) * col_amount + c) * local_rows + qi % local_rows
    qpos = positions(q_anchor, block_order).reshape(1, q_total)
    ki = jnp.arange(k_total, dtype=jnp.int32)
    k_anchor = ((ki // local_rows) * row_amount + r) * local_rows + ki % local_rows
    kpos = positions(k_anchor, block_order).reshape(k_total, 1)

    maxima, summed, weighted = stats_call(pair_all, kv_all, qpos, kpos, scaling)
    stacked = jnp.stack([maxima[:, 0], summed[:, 0], weighted[:, 0]])
    gathered = lax.all_to_all(
        jnp.tile(stacked[None], (row_amount, 1, 1, 1)), "row", 0, 0, tiled=True
    )
    top = jnp.max(gathered[:, 0], axis=0)
    factor = jnp.exp(gathered[:, 0] - top[None])
    summed = jnp.sum(gathered[:, 1] * factor, axis=0)
    weighted = jnp.sum(gathered[:, 2] * factor, axis=0)
    logsum = (top + jnp.log(summed)).reshape(H, 1, q_total)
    deltas = (weighted / summed).reshape(H, 1, q_total)

    query_acc, kv_parts = grad_call(pair_all, kv_all, qpos, kpos, logsum, deltas, scaling)
    kv_grad = lax.psum_scatter(kv_parts, "col", scatter_dimension=0, tiled=True)
    key_grad, value_grad = kv_grad[:, :HD], kv_grad[:, HD:]
    exchanged = lax.all_to_all(query_acc, "row", 0, 0, tiled=True)
    query_grad = jnp.sum(exchanged.reshape(row_amount, local_rows, H * HD), axis=0)
    return (
        (query_grad * scaling).astype(jnp.bfloat16),
        (key_grad * scaling).astype(jnp.bfloat16),
        value_grad.astype(jnp.bfloat16),
    )


def local(queries, key_states, value_states, out_grad, block_order):
    scaling = 1.0 / math.sqrt(key_states.shape[1])
    return tile_grid(queries, key_states, value_states, out_grad, block_order, scaling)


def solution(mesh):
    placed = (
        P(("row", "col"), None),
        P(("col", "row"), None),
        P(("col", "row"), None),
        P(("row", "col"), None),
        P(),
    )
    return jax.shard_map(
        local,
        mesh=mesh,
        in_specs=placed,
        out_specs=(P(("row", "col"), None), P(("col", "row"), None), P(("col", "row"), None)),
        check_vma=False,
    )
```

```python
import math
import os

import jax
import jax.numpy as jnp
from jax import lax
from jax.experimental import pallas as pl
from jax.experimental.pallas import tpu as pltpu
from jax.sharding import PartitionSpec as P

H = 8
HD = 128
BLK = 64
TQ = 256
TS = 1024
INTERPRET = bool(os.environ.get("SOL_INTERPRET"))


def positions(token_index, block_order):
    block_index = token_index // BLK
    block_ids = jnp.arange(block_order.shape[0], dtype=jnp.int32)
    matches = block_index[:, None] == block_ids[None, :]
    start = jnp.sum(jnp.where(matches, block_order[None, :], 0), axis=1)
    return start * BLK + token_index % BLK


def _nt(a, b):
    return lax.dot_general(a, b, (((1,), (1,)), ((), ())), preferred_element_type=jnp.float32)


def _tn(a, b):
    return lax.dot_general(a, b, (((0,), (0,)), ((), ())), preferred_element_type=jnp.float32)


def stats_call(pair_all, kv_all, qpos, kpos, scaling):
    q_total = pair_all.shape[0]
    n = kv_all.shape[0]

    def kernel(q_ref, g_ref, k_ref, v_ref, qp_ref, kp_ref, m_ref, l_ref, w_ref):
        s = _nt(k_ref[...], q_ref[...]) * scaling
        vis = kp_ref[...] <= qp_ref[...]
        s = jnp.where(vis, s, -1e30)
        m = jnp.max(s, axis=0, keepdims=True)
        e = jnp.exp(s - jnp.maximum(m, -1e29))
        dp = _nt(v_ref[...], g_ref[...])
        m_ref[...] = m
        l_ref[...] = jnp.sum(e, axis=0, keepdims=True)
        w_ref[...] = jnp.sum(e * dp, axis=0, keepdims=True)

    stat_blk = pl.BlockSpec((None, 1, TS), lambda b, h: (h, 0, b))
    out = jax.ShapeDtypeStruct((H, 1, q_total), jnp.float32)
    return pl.pallas_call(
        kernel,
        grid=(q_total // TS, H),
        in_specs=[
            pl.BlockSpec((TS, HD), lambda b, h: (b, h)),
            pl.BlockSpec((TS, HD), lambda b, h: (b, H + h)),
            pl.BlockSpec((n, HD), lambda b, h: (0, 0)),
            pl.BlockSpec((n, HD), lambda b, h: (0, 1)),
            pl.BlockSpec((1, TS), lambda b, h: (0, b)),
            pl.BlockSpec((n, 1), lambda b, h: (0, 0)),
        ],
        out_specs=[stat_blk, stat_blk, stat_blk],
        out_shape=[out, out, out],
        compiler_params=pltpu.CompilerParams(dimension_semantics=("arbitrary", "arbitrary")),
        interpret=INTERPRET,
    )(pair_all, pair_all, kv_all, kv_all, qpos, kpos)


def grad_call(pair_all, kv_all, qpos, kpos, logsum, deltas, scaling):
    q_total = pair_all.shape[0]
    n = kv_all.shape[0]

    def kernel(q_ref, g_ref, k_ref, v_ref, qp_ref, kp_ref, ls_ref, dl_ref, dq_ref, kv_ref):
        first = (pl.program_id(0) == 0) & (pl.program_id(1) == 0)
        q = q_ref[...]
        g = g_ref[...]
        k = k_ref[...]
        s = _nt(k, q) * scaling
        vis = kp_ref[...] <= qp_ref[...]
        p = jnp.exp(jnp.where(vis, s, -1e30) - ls_ref[...])
        dp = _nt(v_ref[...], g)
        ds = (p * (dp - dl_ref[...])).astype(jnp.bfloat16)
        pb = p.astype(jnp.bfloat16)
        dq_ref[...] = _tn(ds, k)

        @pl.when(first)
        def _():
            kv_ref[...] = jnp.zeros_like(kv_ref)

        kv_ref[:, :HD] += jnp.dot(ds, q, preferred_element_type=jnp.float32)
        kv_ref[:, HD:] += jnp.dot(pb, g, preferred_element_type=jnp.float32)

    stat_blk = pl.BlockSpec((None, 1, TQ), lambda b, h: (h, 0, b))
    return pl.pallas_call(
        kernel,
        grid=(q_total // TQ, H),
        in_specs=[
            pl.BlockSpec((TQ, HD), lambda b, h: (b, h)),
            pl.BlockSpec((TQ, HD), lambda b, h: (b, H + h)),
            pl.BlockSpec((n, HD), lambda b, h: (0, 0)),
            pl.BlockSpec((n, HD), lambda b, h: (0, 1)),
            pl.BlockSpec((1, TQ), lambda b, h: (0, b)),
            pl.BlockSpec((n, 1), lambda b, h: (0, 0)),
            stat_blk,
            stat_blk,
        ],
        out_specs=[
            pl.BlockSpec((TQ, HD), lambda b, h: (b, h)),
            pl.BlockSpec((n, 2 * HD), lambda b, h: (0, 0)),
        ],
        out_shape=[
            jax.ShapeDtypeStruct((q_total, H * HD), jnp.float32),
            jax.ShapeDtypeStruct((n, 2 * HD), jnp.float32),
        ],
        compiler_params=pltpu.CompilerParams(dimension_semantics=("arbitrary", "arbitrary")),
        interpret=INTERPRET,
    )(pair_all, pair_all, kv_all, kv_all, qpos, kpos, logsum, deltas)


def tile_grid(queries, key_states, value_states, out_grad, block_order, scaling):
    row_amount = lax.axis_size("row")
    col_amount = lax.axis_size("col")
    r = lax.axis_index("row")
    c = lax.axis_index("col")
    local_rows = queries.shape[0]
    pair = jnp.concatenate([queries, out_grad], axis=1)
    pair_all = lax.all_to_all(jnp.tile(pair, (row_amount, 1)), "row", 0, 0, tiled=True)
    kv_all = lax.all_gather(
        jnp.concatenate([key_states, value_states], axis=1), "col", axis=0, tiled=True
    )
    q_total = pair_all.shape[0]
    k_total = kv_all.shape[0]

    qi = jnp.arange(q_total, dtype=jnp.int32)
    q_anchor = ((qi // local_rows) * col_amount + c) * local_rows + qi % local_rows
    qpos = positions(q_anchor, block_order).reshape(1, q_total)
    ki = jnp.arange(k_total, dtype=jnp.int32)
    k_anchor = ((ki // local_rows) * row_amount + r) * local_rows + ki % local_rows
    kpos = positions(k_anchor, block_order).reshape(k_total, 1)

    maxima, summed, weighted = stats_call(pair_all, kv_all, qpos, kpos, scaling)
    stacked = jnp.stack([maxima[:, 0], summed[:, 0], weighted[:, 0]])
    gathered = lax.all_to_all(
        jnp.tile(stacked[None], (row_amount, 1, 1, 1)), "row", 0, 0, tiled=True
    )
    top = jnp.max(gathered[:, 0], axis=0)
    factor = jnp.exp(gathered[:, 0] - top[None])
    summed = jnp.sum(gathered[:, 1] * factor, axis=0)
    weighted = jnp.sum(gathered[:, 2] * factor, axis=0)
    logsum = (top + jnp.log(summed)).reshape(H, 1, q_total)
    deltas = (weighted / summed).reshape(H, 1, q_total)

    query_acc, kv_parts = grad_call(pair_all, kv_all, qpos, kpos, logsum, deltas, scaling)
    kv_grad = lax.psum_scatter(kv_parts, "col", scatter_dimension=0, tiled=True)
    key_grad, value_grad = kv_grad[:, :HD], kv_grad[:, HD:]
    exchanged = lax.all_to_all(query_acc, "row", 0, 0, tiled=True)
    query_grad = jnp.sum(exchanged.reshape(row_amount, local_rows, H * HD), axis=0)
    return (
        (query_grad * scaling).astype(jnp.bfloat16),
        (key_grad * scaling).astype(jnp.bfloat16),
        value_grad.astype(jnp.bfloat16),
    )


def local(queries, key_states, value_states, out_grad, block_order):
    scaling = 1.0 / math.sqrt(key_states.shape[1])
    return tile_grid(queries, key_states, value_states, out_grad, block_order, scaling)


def solution(mesh):
    placed = (
        P(("row", "col"), None),
        P(("col", "row"), None),
        P(("col", "row"), None),
        P(("row", "col"), None),
        P(),
    )
    return jax.shard_map(
        local,
        mesh=mesh,
        in_specs=placed,
        out_specs=(P(("row", "col"), None), P(("col", "row"), None), P(("col", "row"), None)),
        check_vma=False,
    )
```

```python
import math
import os

import jax
import jax.numpy as jnp
from jax import lax
from jax.experimental import pallas as pl
from jax.experimental.pallas import tpu as pltpu
from jax.sharding import PartitionSpec as P

H = 8
HD = 128
BLK = 64
TQ = 256
TS = 1024
INTERPRET = bool(os.environ.get("SOL_INTERPRET"))


def positions(token_index, block_order):
    block_index = token_index // BLK
    block_ids = jnp.arange(block_order.shape[0], dtype=jnp.int32)
    matches = block_index[:, None] == block_ids[None, :]
    start = jnp.sum(jnp.where(matches, block_order[None, :], 0), axis=1)
    return start * BLK + token_index % BLK


def _nt(a, b):
    return lax.dot_general(a, b, (((1,), (1,)), ((), ())), preferred_element_type=jnp.float32)


def _tn(a, b):
    return lax.dot_general(a, b, (((0,), (0,)), ((), ())), preferred_element_type=jnp.float32)


def stats_call(pair_all, kv_all, qpos, kpos, scaling):
    q_total = pair_all.shape[0]
    n = kv_all.shape[0]

    def kernel(q_ref, g_ref, k_ref, v_ref, qp_ref, kp_ref, m_ref, l_ref, w_ref, bias_ref):
        @pl.when(pl.program_id(1) == 0)
        def _():
            bias_ref[...] = jnp.where(kp_ref[...] <= qp_ref[...], 0.0, -1e30)

        s = _nt(k_ref[...], q_ref[...]) * scaling + bias_ref[...]
        m = jnp.max(s, axis=0, keepdims=True)
        e = jnp.exp(s - jnp.maximum(m, -1e29))
        dp = _nt(v_ref[...], g_ref[...])
        m_ref[...] = m
        l_ref[...] = jnp.sum(e, axis=0, keepdims=True)
        w_ref[...] = jnp.sum(e * dp, axis=0, keepdims=True)

    stat_blk = pl.BlockSpec((None, 1, TS), lambda b, h: (h, 0, b))
    out = jax.ShapeDtypeStruct((H, 1, q_total), jnp.float32)
    return pl.pallas_call(
        kernel,
        grid=(q_total // TS, H),
        in_specs=[
            pl.BlockSpec((TS, HD), lambda b, h: (b, h)),
            pl.BlockSpec((TS, HD), lambda b, h: (b, H + h)),
            pl.BlockSpec((n, HD), lambda b, h: (0, 0)),
            pl.BlockSpec((n, HD), lambda b, h: (0, 1)),
            pl.BlockSpec((1, TS), lambda b, h: (0, b)),
            pl.BlockSpec((n, 1), lambda b, h: (0, 0)),
        ],
        out_specs=[stat_blk, stat_blk, stat_blk],
        out_shape=[out, out, out],
        scratch_shapes=[pltpu.VMEM((n, TS), jnp.float32)],
        compiler_params=pltpu.CompilerParams(dimension_semantics=("arbitrary", "arbitrary")),
        interpret=INTERPRET,
    )(pair_all, pair_all, kv_all, kv_all, qpos, kpos)


def grad_call(pair_all, kv_all, qpos, kpos, logsum, deltas, scaling):
    q_total = pair_all.shape[0]
    n = kv_all.shape[0]

    def kernel(q_ref, g_ref, k_ref, v_ref, qp_ref, kp_ref, ls_ref, dl_ref, dq_ref, kv_ref, bias_ref):
        first = (pl.program_id(0) == 0) & (pl.program_id(1) == 0)

        @pl.when(pl.program_id(1) == 0)
        def _():
            bias_ref[...] = jnp.where(kp_ref[...] <= qp_ref[...], 0.0, -1e30)

        q = q_ref[...]
        g = g_ref[...]
        k = k_ref[...]
        s = _nt(k, q) * scaling + bias_ref[...]
        p = jnp.exp(s - ls_ref[...])
        dp = _nt(v_ref[...], g)
        ds = (p * (dp - dl_ref[...])).astype(jnp.bfloat16)
        pb = p.astype(jnp.bfloat16)
        dq_ref[...] = _tn(ds, k)

        @pl.when(first)
        def _():
            kv_ref[...] = jnp.zeros_like(kv_ref)

        kv_ref[:, :HD] += jnp.dot(ds, q, preferred_element_type=jnp.float32)
        kv_ref[:, HD:] += jnp.dot(pb, g, preferred_element_type=jnp.float32)

    stat_blk = pl.BlockSpec((None, 1, TQ), lambda b, h: (h, 0, b))
    return pl.pallas_call(
        kernel,
        grid=(q_total // TQ, H),
        in_specs=[
            pl.BlockSpec((TQ, HD), lambda b, h: (b, h)),
            pl.BlockSpec((TQ, HD), lambda b, h: (b, H + h)),
            pl.BlockSpec((n, HD), lambda b, h: (0, 0)),
            pl.BlockSpec((n, HD), lambda b, h: (0, 1)),
            pl.BlockSpec((1, TQ), lambda b, h: (0, b)),
            pl.BlockSpec((n, 1), lambda b, h: (0, 0)),
            stat_blk,
            stat_blk,
        ],
        out_specs=[
            pl.BlockSpec((TQ, HD), lambda b, h: (b, h)),
            pl.BlockSpec((n, 2 * HD), lambda b, h: (0, 0)),
        ],
        out_shape=[
            jax.ShapeDtypeStruct((q_total, H * HD), jnp.float32),
            jax.ShapeDtypeStruct((n, 2 * HD), jnp.float32),
        ],
        scratch_shapes=[pltpu.VMEM((n, TQ), jnp.float32)],
        compiler_params=pltpu.CompilerParams(dimension_semantics=("arbitrary", "arbitrary")),
        interpret=INTERPRET,
    )(pair_all, pair_all, kv_all, kv_all, qpos, kpos, logsum, deltas)


def tile_grid(queries, key_states, value_states, out_grad, block_order, scaling):
    row_amount = lax.axis_size("row")
    col_amount = lax.axis_size("col")
    r = lax.axis_index("row")
    c = lax.axis_index("col")
    local_rows = queries.shape[0]
    pair = jnp.concatenate([queries, out_grad], axis=1)
    pair_all = lax.all_to_all(jnp.tile(pair, (row_amount, 1)), "row", 0, 0, tiled=True)
    kv_all = lax.all_gather(
        jnp.concatenate([key_states, value_states], axis=1), "col", axis=0, tiled=True
    )
    q_total = pair_all.shape[0]
    k_total = kv_all.shape[0]

    qi = jnp.arange(q_total, dtype=jnp.int32)
    q_anchor = ((qi // local_rows) * col_amount + c) * local_rows + qi % local_rows
    qpos = positions(q_anchor, block_order).reshape(1, q_total)
    ki = jnp.arange(k_total, dtype=jnp.int32)
    k_anchor = ((ki // local_rows) * row_amount + r) * local_rows + ki % local_rows
    kpos = positions(k_anchor, block_order).reshape(k_total, 1)

    maxima, summed, weighted = stats_call(pair_all, kv_all, qpos, kpos, scaling)
    stacked = jnp.stack([maxima[:, 0], summed[:, 0], weighted[:, 0]])
    gathered = lax.all_to_all(
        jnp.tile(stacked[None], (row_amount, 1, 1, 1)), "row", 0, 0, tiled=True
    )
    top = jnp.max(gathered[:, 0], axis=0)
    factor = jnp.exp(gathered[:, 0] - top[None])
    summed = jnp.sum(gathered[:, 1] * factor, axis=0)
    weighted = jnp.sum(gathered[:, 2] * factor, axis=0)
    logsum = (top + jnp.log(summed)).reshape(H, 1, q_total)
    deltas = (weighted / summed).reshape(H, 1, q_total)

    query_acc, kv_parts = grad_call(pair_all, kv_all, qpos, kpos, logsum, deltas, scaling)
    kv_grad = lax.psum_scatter(kv_parts, "col", scatter_dimension=0, tiled=True)
    key_grad, value_grad = kv_grad[:, :HD], kv_grad[:, HD:]
    exchanged = lax.all_to_all(query_acc, "row", 0, 0, tiled=True)
    query_grad = jnp.sum(exchanged.reshape(row_amount, local_rows, H * HD), axis=0)
    return (
        (query_grad * scaling).astype(jnp.bfloat16),
        (key_grad * scaling).astype(jnp.bfloat16),
        value_grad.astype(jnp.bfloat16),
    )


def local(queries, key_states, value_states, out_grad, block_order):
    scaling = 1.0 / math.sqrt(key_states.shape[1])
    return tile_grid(queries, key_states, value_states, out_grad, block_order, scaling)


def solution(mesh):
    placed = (
        P(("row", "col"), None),
        P(("col", "row"), None),
        P(("col", "row"), None),
        P(("row", "col"), None),
        P(),
    )
    return jax.shard_map(
        local,
        mesh=mesh,
        in_specs=placed,
        out_specs=(P(("row", "col"), None), P(("col", "row"), None), P(("col", "row"), None)),
        check_vma=False,
    )
```

```python
import math
import os

import jax
import jax.numpy as jnp
from jax import lax
from jax.experimental import pallas as pl
from jax.experimental.pallas import tpu as pltpu
from jax.sharding import PartitionSpec as P

H = 8
HD = 128
BLK = 64
TQ = 256
TS = 1024
INTERPRET = bool(os.environ.get("SOL_INTERPRET"))


def positions(token_index, block_order):
    block_index = token_index // BLK
    block_ids = jnp.arange(block_order.shape[0], dtype=jnp.int32)
    matches = block_index[:, None] == block_ids[None, :]
    start = jnp.sum(jnp.where(matches, block_order[None, :], 0), axis=1)
    return start * BLK + token_index % BLK


def _nt(a, b):
    return lax.dot_general(a, b, (((1,), (1,)), ((), ())), preferred_element_type=jnp.float32)


def _tn(a, b):
    return lax.dot_general(a, b, (((0,), (0,)), ((), ())), preferred_element_type=jnp.float32)


def stats_call(pair_all, kv_all, qpos, kpos, scaling):
    q_total = pair_all.shape[0]
    n = kv_all.shape[0]

    def kernel(q_ref, g_ref, k_ref, v_ref, qp_ref, kp_ref, m_ref, l_ref, w_ref, bias_ref):
        @pl.when(pl.program_id(1) == 0)
        def _():
            bias_ref[...] = jnp.where(kp_ref[...] <= qp_ref[...], 0.0, -1e30)

        s = _nt(k_ref[...], q_ref[...]) * scaling + bias_ref[...]
        m = jnp.max(s, axis=0, keepdims=True)
        e = jnp.exp(s - jnp.maximum(m, -1e29))
        dp = _nt(v_ref[...], g_ref[...])
        m_ref[...] = m
        l_ref[...] = jnp.sum(e, axis=0, keepdims=True)
        w_ref[...] = jnp.sum(e * dp, axis=0, keepdims=True)

    stat_blk = pl.BlockSpec((None, 1, TS), lambda b, h: (h, 0, b))
    out = jax.ShapeDtypeStruct((H, 1, q_total), jnp.float32)
    return pl.pallas_call(
        kernel,
        grid=(q_total // TS, H),
        in_specs=[
            pl.BlockSpec((TS, HD), lambda b, h: (b, h)),
            pl.BlockSpec((TS, HD), lambda b, h: (b, H + h)),
            pl.BlockSpec((n, HD), lambda b, h: (0, 0)),
            pl.BlockSpec((n, HD), lambda b, h: (0, 1)),
            pl.BlockSpec((1, TS), lambda b, h: (0, b)),
            pl.BlockSpec((n, 1), lambda b, h: (0, 0)),
        ],
        out_specs=[stat_blk, stat_blk, stat_blk],
        out_shape=[out, out, out],
        scratch_shapes=[pltpu.VMEM((n, TS), jnp.float32)],
        compiler_params=pltpu.CompilerParams(dimension_semantics=("arbitrary", "arbitrary")),
        interpret=INTERPRET,
    )(pair_all, pair_all, kv_all, kv_all, qpos, kpos)


def grad_call(pair_all, kv_all, key_t, qpos, kpos, logsum, deltas, scaling):
    q_total = pair_all.shape[0]
    n = kv_all.shape[0]

    def kernel(q_ref, g_ref, k_ref, v_ref, kt_ref, qp_ref, kp_ref, ls_ref, dl_ref, dq_ref, kv_ref, bias_ref):
        first = (pl.program_id(0) == 0) & (pl.program_id(1) == 0)

        @pl.when(pl.program_id(1) == 0)
        def _():
            bias_ref[...] = jnp.where(kp_ref[...] <= qp_ref[...], 0.0, -1e30)

        q = q_ref[...]
        g = g_ref[...]
        k = k_ref[...]
        s = _nt(k, q) * scaling + bias_ref[...]
        p = jnp.exp(s - ls_ref[...])
        dp = _nt(v_ref[...], g)
        ds = (p * (dp - dl_ref[...])).astype(jnp.bfloat16)
        pb = p.astype(jnp.bfloat16)
        dq_ref[...] = jnp.dot(kt_ref[...], ds, preferred_element_type=jnp.float32)

        @pl.when(first)
        def _():
            kv_ref[...] = jnp.zeros_like(kv_ref)

        kv_ref[:, :HD] += jnp.dot(ds, q, preferred_element_type=jnp.float32)
        kv_ref[:, HD:] += jnp.dot(pb, g, preferred_element_type=jnp.float32)

    stat_blk = pl.BlockSpec((None, 1, TQ), lambda b, h: (h, 0, b))
    return pl.pallas_call(
        kernel,
        grid=(q_total // TQ, H),
        in_specs=[
            pl.BlockSpec((TQ, HD), lambda b, h: (b, h)),
            pl.BlockSpec((TQ, HD), lambda b, h: (b, H + h)),
            pl.BlockSpec((n, HD), lambda b, h: (0, 0)),
            pl.BlockSpec((n, HD), lambda b, h: (0, 1)),
            pl.BlockSpec((HD, n), lambda b, h: (0, 0)),
            pl.BlockSpec((1, TQ), lambda b, h: (0, b)),
            pl.BlockSpec((n, 1), lambda b, h: (0, 0)),
            stat_blk,
            stat_blk,
        ],
        out_specs=[
            pl.BlockSpec((HD, TQ), lambda b, h: (h, b)),
            pl.BlockSpec((n, 2 * HD), lambda b, h: (0, 0)),
        ],
        out_shape=[
            jax.ShapeDtypeStruct((H * HD, q_total), jnp.float32),
            jax.ShapeDtypeStruct((n, 2 * HD), jnp.float32),
        ],
        scratch_shapes=[pltpu.VMEM((n, TQ), jnp.float32)],
        compiler_params=pltpu.CompilerParams(dimension_semantics=("arbitrary", "arbitrary")),
        interpret=INTERPRET,
    )(pair_all, pair_all, kv_all, kv_all, key_t, qpos, kpos, logsum, deltas)


def tile_grid(queries, key_states, value_states, out_grad, block_order, scaling):
    row_amount = lax.axis_size("row")
    col_amount = lax.axis_size("col")
    r = lax.axis_index("row")
    c = lax.axis_index("col")
    local_rows = queries.shape[0]
    pair = jnp.concatenate([queries, out_grad], axis=1)
    pair_all = lax.all_to_all(jnp.tile(pair, (row_amount, 1)), "row", 0, 0, tiled=True)
    kv_all = lax.all_gather(
        jnp.concatenate([key_states, value_states], axis=1), "col", axis=0, tiled=True
    )
    q_total = pair_all.shape[0]
    k_total = kv_all.shape[0]

    qi = jnp.arange(q_total, dtype=jnp.int32)
    q_anchor = ((qi // local_rows) * col_amount + c) * local_rows + qi % local_rows
    qpos = positions(q_anchor, block_order).reshape(1, q_total)
    ki = jnp.arange(k_total, dtype=jnp.int32)
    k_anchor = ((ki // local_rows) * row_amount + r) * local_rows + ki % local_rows
    kpos = positions(k_anchor, block_order).reshape(k_total, 1)

    maxima, summed, weighted = stats_call(pair_all, kv_all, qpos, kpos, scaling)
    stacked = jnp.stack([maxima[:, 0], summed[:, 0], weighted[:, 0]])
    gathered = lax.all_to_all(
        jnp.tile(stacked[None], (row_amount, 1, 1, 1)), "row", 0, 0, tiled=True
    )
    top = jnp.max(gathered[:, 0], axis=0)
    factor = jnp.exp(gathered[:, 0] - top[None])
    summed = jnp.sum(gathered[:, 1] * factor, axis=0)
    weighted = jnp.sum(gathered[:, 2] * factor, axis=0)
    logsum = (top + jnp.log(summed)).reshape(H, 1, q_total)
    deltas = (weighted / summed).reshape(H, 1, q_total)

    key_t = kv_all[:, :HD].T
    query_t, kv_parts = grad_call(pair_all, kv_all, key_t, qpos, kpos, logsum, deltas, scaling)
    query_acc = query_t.T
    kv_grad = lax.psum_scatter(kv_parts, "col", scatter_dimension=0, tiled=True)
    key_grad, value_grad = kv_grad[:, :HD], kv_grad[:, HD:]
    exchanged = lax.all_to_all(query_acc, "row", 0, 0, tiled=True)
    query_grad = jnp.sum(exchanged.reshape(row_amount, local_rows, H * HD), axis=0)
    return (
        (query_grad * scaling).astype(jnp.bfloat16),
        (key_grad * scaling).astype(jnp.bfloat16),
        value_grad.astype(jnp.bfloat16),
    )


def local(queries, key_states, value_states, out_grad, block_order):
    scaling = 1.0 / math.sqrt(key_states.shape[1])
    return tile_grid(queries, key_states, value_states, out_grad, block_order, scaling)


def solution(mesh):
    placed = (
        P(("row", "col"), None),
        P(("col", "row"), None),
        P(("col", "row"), None),
        P(("row", "col"), None),
        P(),
    )
    return jax.shard_map(
        local,
        mesh=mesh,
        in_specs=placed,
        out_specs=(P(("row", "col"), None), P(("col", "row"), None), P(("col", "row"), None)),
        check_vma=False,
    )
```
